32 devices in a mesh: path: 4 (over y, x), head: 2 (over core), expert: 4 (over z).
Axes of the slice: x: 2, y: 2, z: 4, core: 2. Of those that a mesh axis runs over, the one named last changes fastest.
Arguments:
- tokens: bfloat16 [4096, 2048], P(('path', 'expert'), 'head'), may hold values from -6 to 6
- routes: int32 [4096, 2], P(('path', 'expert')), may hold values from 0 to 15, all different within a row; in each aligned block of 256 rows (0 to 255, 256 to 511, ...) at most 64 rows name the same one
- combine_weights: float32 [4096, 2], P(('path', 'expert')), may hold values from 0.1 to 0.9
- w_gate: bfloat16 [16, 2048, 768], P(('path', 'expert'), None, 'head'), may hold values from -0.125 to 0.125
- w_up: bfloat16 [16, 2048, 768], P(('path', 'expert'), None, 'head'), may hold values from -0.125 to 0.125
- w_down: bfloat16 [16, 768, 2048], P(('path', 'expert'), 'head'), may hold values from -0.21875 to 0.21875
- cotangent: bfloat16 [4096, 2048], P(('path', 'expert'), 'head'), may hold values from -1.5 to 1.5
Outputs:
- layer_out: bfloat16 [4096, 2048], P(('path', 'expert'), 'head')
- d_tokens: bfloat16 [4096, 2048], P(('path', 'expert'), 'head')
- d_gates: float32 [4096, 2], P(('path', 'expert'))
- grad_gate: bfloat16 [16, 2048, 768], P(('path', 'expert'), None, 'head')
- grad_up: bfloat16 [16, 2048, 768], P(('path', 'expert'), None, 'head')
- grad_down: bfloat16 [16, 768, 2048], P(('path', 'expert'), 'head')
The draws below stay inside these ranges and needn't reach their ends.
Inputs may be any that keep to these rules, and one draw needn't show every extreme that they name: `routes`: each row names 2 different experts. Within the 256 rows of one device (aligned blocks) no expert is named more than 64 times, and in every draw some expert is named exactly 64 times within some block.
All inputs are finite; a program needn't handle non-finite values.
Results may differ from the reference program's by a relative error of at most 0.0072.
Values may be sent and summed in bfloat16 or wider, within the bound.
No kernel may reach another device: no remote copies, remote signals or barrier semaphores. Data moves between devices by JAX's collectives and lax.ppermute only.
A program may use at most 128 MiB of HBM per device.

```python
import math
import jax
import jax.numpy as jnp
import numpy as np
from jax import lax

D = 2048
FF = 768
TOP = 2
EXPERTS = 16
TOK_DEV = 256
TOKENS = 4096
CAP = 64
N_PATH = 4
N_HEAD = 2
N_EXPERT = 4


def shard_levels(stream_key, dims, pieces, smallest, largest):
    def one(dim, blocks):
        draws = jax.random.uniform(jax.random.fold_in(jax.random.fold_in(stream_key, 6), dim), (blocks,), jnp.float32, smallest / len(pieces), largest / len(pieces))
        return jnp.repeat(jnp.exp(draws), dims[dim] // blocks).reshape((-1,) + (1,) * (len(dims) - dim - 1))

    gain = one(*pieces[0])
    for cut in pieces[1:]:
        gain = gain * one(*cut)
    return gain


def deal_out(stream_key, own, number, rows, amount, top, bound, slope):
    ranking = jax.random.permutation(stream_key, amount)
    packed, ordinary = portions_of(amount, rows * top, bound, slope, True), portions_of(amount, rows * top, bound, slope, False)
    places = jnp.arange(amount)

    def named(lengths, offset_by):
        used = int((lengths > 0).sum())
        fixed = max(1, used // 4)
        shifted = fixed + (places - fixed + offset_by * (used - fixed)) % max(1, amount - fixed)
        return jnp.zeros((amount,), jnp.int32).at[ranking[jnp.where(places < fixed, places, shifted)]].set(jnp.asarray(lengths, jnp.int32))

    lengths = jnp.where(number % 4 == 0, named(packed, number // 4), named(ordinary, number - number // 4 - 1))
    mixed = jax.random.permutation(jax.random.fold_in(own, 3), amount)
    donor, sink = mixed[0:amount // 2 * 2:2], mixed[1:amount // 2 * 2:2]
    room = jnp.minimum(lengths[donor] - 1, bound - lengths[sink]) // 2
    room = jnp.where((donor == ranking[0]) | (sink == ranking[0]) | (lengths[sink] == 0), 0, jnp.maximum(room, 0))
    shifted = jax.random.randint(jax.random.fold_in(own, 4), (amount // 2,), 0, 1 << 20) % (room + 1)
    lengths = lengths.at[donor].add(-shifted).at[sink].add(shifted)
    labels = jnp.searchsorted(jnp.cumsum(lengths), jnp.arange(rows * top), side="right").astype(jnp.int32)
    grid = labels.reshape(top, rows).T
    grid = grid[jax.random.permutation(jax.random.fold_in(own, 1), rows)]
    offset_by = jax.random.randint(jax.random.fold_in(own, 2), (rows, 1), 0, top)
    return jnp.take_along_axis(grid, (jnp.arange(top)[None, :] + offset_by) % top, axis=1)


def portions_of(count, total, bound, slope, full):
    weights = [(1 << 20) // math.isqrt(grade ** slope) + 1 for grade in range(1, count + 1)]
    largest = bound if full else min(bound, max(-(-total // count), total * weights[0] // sum(weights)))
    least = 1 if total - largest >= count - 1 else 0
    holding, rest = [largest] + [least] * (count - 1), total - largest - least * (count - 1)
    while rest > 0:
        movable = [i for i in range(1, count) if holding[i] < largest] or [i for i in range(1, count) if holding[i] < bound]
        mass, remaining = sum([weights[i] for i in movable]), rest
        for i in movable:
            more = min(bound - holding[i], max(1, remaining * weights[i] // mass), rest)
            holding[i] = holding[i] + more
            rest = rest - more
    return np.array(holding)


def centred(rng, dims, deviation, limit, cuts=(), held_as=jnp.bfloat16):
    drawn = jax.random.normal(rng, dims, jnp.float32) * deviation
    if len(cuts) > 0:
        drawn = shard_levels(rng, dims, cuts, -0.22, 0.18) * drawn
    return jnp.clip(drawn, min=-limit, max=limit).astype(held_as)


def setup_inputs(seed: int = 0) -> dict:
    splits = jax.random.split(jax.random.key(seed), 8)
    tokens = centred(splits[0], (TOKENS, D), 1.0, 6.0, ((0, 16), (1, 2)))
    routes_keys = jax.random.split(jax.random.fold_in(splits[1], 1), TOKENS // TOK_DEV)
    routes_turns = jax.random.permutation(jax.random.fold_in(splits[1], 3), TOKENS // TOK_DEV)
    routes = jax.vmap(lambda own, number: deal_out(jax.random.fold_in(splits[1], 2), own, number, TOK_DEV, EXPERTS, TOP, CAP, 2))(routes_keys, routes_turns).reshape((TOKENS, TOP))
    combine_weights = jnp.clip(0.1 + 0.79999997 * jax.random.uniform(splits[2], (TOKENS, TOP), jnp.float32) ** shard_levels(splits[2], (TOKENS, TOP), ((0, 16),), -0.2, 0.2), 0.1, 0.9)
    w_gate = centred(splits[3], (EXPERTS, D, FF), D ** -0.5, 0.125, ((0, 16), (2, 2)))
    w_up = centred(splits[4], (EXPERTS, D, FF), D ** -0.5, 0.125, ((0, 16), (2, 2)))
    w_down = centred(splits[5], (EXPERTS, FF, D), FF ** -0.5, 0.21875, ((0, 16), (1, 2)))
    cotangent = centred(splits[6], (TOKENS, D), 0.25, 1.5, ((0, 16), (1, 2)))
    return {"tokens": tokens, "routes": routes, "combine_weights": combine_weights, "w_gate": w_gate, "w_up": w_up, "w_down": w_down, "cotangent": cotangent}


def rounded(values):
    return lax.optimization_barrier(values.astype(jnp.bfloat16)).astype(jnp.float32)


def one_expert(expert_items):
    inbound, grad_in, gate_w, up_w, down_w = expert_items
    model_width = gate_w.shape[0]
    block_width = gate_w.shape[1] // N_HEAD
    pre_gate = jnp.dot(inbound, gate_w, preferred_element_type=jnp.float32)
    pre_up = jnp.dot(inbound, up_w, preferred_element_type=jnp.float32)
    activation = (jax.nn.silu(pre_gate) * pre_up).astype(jnp.bfloat16)
    act_blocks = activation.astype(jnp.float32).reshape(-1, N_HEAD, block_width)
    down_blocks = down_w.astype(jnp.float32).reshape(N_HEAD, block_width, model_width)
    parts = jnp.einsum("shf,hfd->hsd", act_blocks, down_blocks, precision=lax.Precision.HIGHEST)
    expert_out = jnp.sum(rounded(parts), axis=0).astype(jnp.bfloat16)
    d_act = lax.dot_general(grad_in, down_w, (((1,), (1,)), ((), ())), preferred_element_type=jnp.float32)
    sigmoid_gate = jax.nn.sigmoid(pre_gate)
    d_pre_gate = (d_act * pre_up * sigmoid_gate * (1.0 + pre_gate * (1.0 - sigmoid_gate))).astype(jnp.bfloat16)
    d_pre_up = (d_act * jax.nn.silu(pre_gate)).astype(jnp.bfloat16)
    grad_gate = lax.dot_general(inbound, d_pre_gate, (((0,), (0,)), ((), ())), preferred_element_type=jnp.float32).astype(jnp.bfloat16)
    grad_up = lax.dot_general(inbound, d_pre_up, (((0,), (0,)), ((), ())), preferred_element_type=jnp.float32).astype(jnp.bfloat16)
    grad_down = lax.dot_general(activation, grad_in, (((0,), (0,)), ((), ())), preferred_element_type=jnp.float32).astype(jnp.bfloat16)
    gate_blocks = gate_w.astype(jnp.float32).reshape(model_width, N_HEAD, block_width)
    up_blocks = up_w.astype(jnp.float32).reshape(model_width, N_HEAD, block_width)
    dgate_blocks = d_pre_gate.astype(jnp.float32).reshape(-1, N_HEAD, block_width)
    dup_blocks = d_pre_up.astype(jnp.float32).reshape(-1, N_HEAD, block_width)
    back_parts = jnp.einsum("shf,dhf->hsd", dgate_blocks, gate_blocks, precision=lax.Precision.HIGHEST) + jnp.einsum("shf,dhf->hsd", dup_blocks, up_blocks, precision=lax.Precision.HIGHEST)
    back_out = jnp.sum(rounded(back_parts), axis=0).astype(jnp.bfloat16)
    return expert_out, back_out, grad_gate, grad_up, grad_down


def reference(tokens, routes, combine_weights, w_gate, w_up, w_down, cotangent):
    groups = N_PATH * N_EXPERT
    model_width = tokens.shape[1]
    group_rows = TOK_DEV * TOP
    per_expert = groups * CAP
    slot_total = EXPERTS * per_expert
    flat_routes = routes.reshape(groups, group_rows)
    onehot = (flat_routes[:, :, None] == jnp.arange(EXPERTS, dtype=jnp.int32)[None, None, :]).astype(jnp.int32)
    before = jnp.cumsum(onehot, axis=1) - onehot
    slot_index = jnp.sum(before * onehot, axis=2).astype(jnp.int32)
    source = jnp.arange(groups, dtype=jnp.int32)[:, None]
    position = (flat_routes * per_expert + source * CAP + slot_index).reshape(-1).astype(jnp.int32)
    repeated = jnp.repeat(tokens, TOP, axis=0)
    cot_float = cotangent.astype(jnp.float32)
    scaled = (combine_weights[:, :, None] * cot_float[:, None, :]).astype(jnp.bfloat16).reshape(-1, model_width)
    token_buffer = jnp.zeros((slot_total, model_width), jnp.bfloat16).at[position].set(repeated).reshape(EXPERTS, per_expert, model_width)
    grad_buffer = jnp.zeros((slot_total, model_width), jnp.bfloat16).at[position].set(scaled).reshape(EXPERTS, per_expert, model_width)
    out_buffer, back_buffer, grad_gate, grad_up, grad_down = lax.map(one_expert, (token_buffer, grad_buffer, w_gate, w_up, w_down))
    expert_out = out_buffer.reshape(slot_total, model_width)[position].reshape(-1, TOP, model_width).astype(jnp.float32)
    back_out = back_buffer.reshape(slot_total, model_width)[position].reshape(-1, TOP, model_width).astype(jnp.float32)
    layer_out = jnp.sum(combine_weights[:, :, None] * expert_out, axis=1).astype(jnp.bfloat16)
    d_gates = jnp.sum(cot_float[:, None, :] * expert_out, axis=2)
    d_tokens = jnp.sum(back_out, axis=1).astype(jnp.bfloat16)
    return layer_out, d_tokens, d_gates, grad_gate, grad_up, grad_down
```

```python
import jax
import jax.numpy as jnp
from jax import lax
from jax.sharding import PartitionSpec as P

BF = jnp.bfloat16
F32 = jnp.float32


def dot(a, b, ca, cb):
    return lax.dot_general(a, b, (((ca,), (cb,)), ((), ())), preferred_element_type=F32)


def arrivals(line):
    table = []
    for place in range(line):
        order = []
        for dist in range(1, line):
            if place - dist >= 0:
                order.append((0, dist))
            if place + dist < line:
                order.append((1, dist))
        table.append(order)
    return table


def by_place(place, options):
    chosen = options[0]
    seen = [options[0]]
    for option in options[1:]:
        if any(option is other for other in seen):
            continue
        seen.append(option)
        hit = False
        for index, other in enumerate(options):
            if other is option:
                hit = (place == index) | hit
        chosen = jnp.where(hit, option, chosen)
    return chosen


def line_gather(block, line):
    left, right = [block], [block]
    for dist in range(1, line):
        left.append(
            lax.ppermute(left[-1], "expert", [(i, i + 1) for i in range(dist - 1, line - 1)])
        )
        right.append(
            lax.ppermute(right[-1], "expert", [(i + 1, i) for i in range(0, line - dist)])
        )
    return (left, right)


def line_reduce(parts, own, line, table, place, dtype):
    zero = jnp.zeros_like(own)
    right = left = None
    for dist in range(line - 1, 0, -1):
        to_right = by_place(
            place,
            [
                parts[table[i].index((1, dist))] if (1, dist) in table[i] else zero
                for i in range(line)
            ],
        )
        to_left = by_place(
            place,
            [
                parts[table[i].index((0, dist))] if (0, dist) in table[i] else zero
                for i in range(line)
            ],
        )
        if right is not None:
            to_right = to_right + right.astype(F32)
            to_left = to_left + left.astype(F32)
        right = lax.ppermute(
            to_right.astype(dtype), "expert", [(i, i + 1) for i in range(0, line - dist)]
        )
        left = lax.ppermute(
            to_left.astype(dtype), "expert", [(i, i - 1) for i in range(dist, line)]
        )
    return own + right.astype(F32) + left.astype(F32)


def shards(tokens, routes, combine_weights, w_gate, w_up, w_down, cotangent):
    columns, line = lax.axis_size("path"), lax.axis_size("expert")
    column, place, head = lax.axis_index("path"), lax.axis_index("expert"), lax.axis_index("head")
    tok_rows, half = tokens.shape
    top = routes.shape[1]
    groups = columns * line
    cap = max(2, 2 * tok_rows * top // groups)
    slots = columns * cap
    table = arrivals(line)
    swap = [(0, 1), (1, 0)]

    flat = routes.reshape(-1)
    order = jnp.arange(flat.shape[0], dtype=jnp.int32)
    earlier = (flat[:, None] == flat[None, :]) & (order[:, None] < order[None, :])
    rank = jnp.sum(earlier.astype(jnp.int32), axis=0)
    position = (flat * cap + rank).astype(F32).reshape(tok_rows, top)
    about = jnp.concatenate([position.T, combine_weights.T], axis=0)

    about_in = line_gather(about, line)
    tok_in = line_gather(tokens, line)
    cot_in = line_gather(cotangent, line)

    def batch(arrived, own, j):
        if j == 0:
            return own
        options = [arrived[table[i][j - 1][0]][table[i][j - 1][1]] for i in range(line)]
        return by_place(place, options)

    def exchange(pieces):
        return [pieces[0]] + [
            lax.ppermute(pieces[d], "path", [(i, i ^ d) for i in range(columns)])
            for d in range(1, columns)
        ]

    picks, weights, own_cots, tok_rows_in, cot_rows_in = [], [], [], [], []
    slot_ids = lax.broadcasted_iota(jnp.int32, (slots, tok_rows), 0)
    for j in range(line):
        info = batch(about_in, about, j)
        here, weighted = [], 0.0
        for k in range(top):
            where_to = info[k].astype(jnp.int32)
            expert = where_to // cap
            slot = ((expert // line) ^ column) * cap + where_to % cap
            slot = jnp.where(expert % line == place, slot, -1)
            hit = slot_ids == slot[None, :]
            here.append(hit)
            weighted = weighted + jnp.where(hit, info[top + k][None, :], 0.0)
        any_hit = here[0]
        for hit in here[1:]:
            any_hit = any_hit | hit
        pick = any_hit.astype(BF)
        slot_weight = jnp.sum(weighted, axis=1, keepdims=True)
        picks.append((pick, here))
        weights.append(weighted)
        tok_block, cot_block = batch(tok_in, tokens, j), batch(cot_in, cotangent, j)
        own_cots.append(cot_block)
        tok_pieces, cot_pieces = [], []
        for d in range(columns):
            span = slice(d * cap, (d + 1) * cap)
            tok_pieces.append(dot(pick[span], tok_block, 1, 0).astype(BF))
            cot_pieces.append((slot_weight[span] * dot(pick[span], cot_block, 1, 0)).astype(BF))
        tok_rows_in += exchange(tok_pieces)
        cot_rows_in += exchange(cot_pieces)

    def full_rows(pieces):
        mine = jnp.concatenate(pieces, axis=0)
        other = lax.ppermute(mine, "head", swap)
        first = head == 0
        return jnp.concatenate(
            [jnp.where(first, mine, other), jnp.where(first, other, mine)], axis=1
        )

    gate_cols, up_cols, down_rows = w_gate[0], w_up[0], w_down[0]
    start, away = head * half, (1 - head) * half

    def head_sum(make):
        kept, sent = make(start), make(away).astype(BF)
        return (kept + lax.ppermute(sent, "head", swap).astype(F32)).astype(BF)

    inbound = full_rows(tok_rows_in)
    pre_gate = dot(inbound, gate_cols, 1, 0)
    pre_up = dot(inbound, up_cols, 1, 0)
    activation = (jax.nn.silu(pre_gate) * pre_up).astype(BF)
    out_rows = head_sum(
        lambda at: dot(activation, lax.dynamic_slice_in_dim(down_rows, at, half, 1), 1, 0)
    )

    grad_in = full_rows(cot_rows_in)
    d_act = dot(grad_in, down_rows, 1, 1)
    sig = jax.nn.sigmoid(pre_gate)
    d_pre_gate = (d_act * pre_up * sig * (1.0 + pre_gate * (1.0 - sig))).astype(BF)
    d_pre_up = (d_act * jax.nn.silu(pre_gate)).astype(BF)
    back_rows = head_sum(
        lambda at: dot(d_pre_gate, lax.dynamic_slice_in_dim(gate_cols, at, half, 0), 1, 1)
        + dot(d_pre_up, lax.dynamic_slice_in_dim(up_cols, at, half, 0), 1, 1)
    )
    grad_gate = dot(inbound, d_pre_gate, 0, 0).astype(BF)
    grad_up = dot(inbound, d_pre_up, 0, 0).astype(BF)
    grad_down = dot(activation, grad_in, 0, 0).astype(BF)

    def home(rows, j):
        base = j * slots
        pieces = [rows[base + d * cap : base + (d + 1) * cap] for d in range(columns)]
        return jnp.concatenate(exchange(pieces), axis=0)

    out_parts, gate_parts, back_parts = [], [], []
    for j in range(line):
        pick, here = picks[j]
        rows = home(out_rows, j)
        high = weights[j].astype(BF)
        low = (weights[j] - high.astype(F32)).astype(BF)
        out_parts.append(dot(high, rows, 0, 0) + dot(low, rows, 0, 0))
        meet = dot(rows, own_cots[j], 1, 1)
        gate_parts.append(
            jnp.stack([jnp.sum(jnp.where(hit, meet, 0.0), axis=0) for hit in here], axis=0)
        )
        back_parts.append(dot(pick, home(back_rows, j), 0, 0))
    layer_out = line_reduce(out_parts[1:], out_parts[0], line, table, place, BF)
    d_tokens = line_reduce(back_parts[1:], back_parts[0], line, table, place, BF)
    local_gates = line_reduce(gate_parts[1:], gate_parts[0], line, table, place, F32)
    d_gates = (local_gates + lax.ppermute(local_gates, "head", swap)).T
    return (
        layer_out.astype(BF),
        d_tokens.astype(BF),
        d_gates,
        grad_gate[None],
        grad_up[None],
        grad_down[None],
    )


def solution(mesh):
    rows = P(("path", "expert"), "head")
    whole = P(("path", "expert"), None)
    cols = P(("path", "expert"), None, "head")
    downs = P(("path", "expert"), "head", None)
    return jax.shard_map(
        shards,
        mesh=mesh,
        in_specs=(rows, whole, whole, cols, cols, downs, rows),
        out_specs=(rows, rows, whole, cols, cols, downs),
        check_vma=False,
    )
```

```python
import functools

import jax
import jax.numpy as jnp
from jax import lax
from jax.experimental import pallas as pl
from jax.experimental.pallas import tpu as pltpu
from jax.sharding import PartitionSpec as P

BF = jnp.bfloat16
F32 = jnp.float32
VMEM = pl.BlockSpec(memory_space=pltpu.VMEM)
SMEM = pl.BlockSpec(memory_space=pltpu.SMEM)
ANY = pl.BlockSpec(memory_space=pl.ANY)
PARAMS = pltpu.CompilerParams(vmem_limit_bytes=48 << 20)
SWAP = [(0, 1), (1, 0)]
SMALL = pl.CostEstimate(flops=0, bytes_accessed=0, transcendentals=0)


def dot(a, b, ca, cb):
    return lax.dot_general(a, b, (((ca,), (cb,)), ((), ())), preferred_element_type=F32)


def powers(line):
    bits = [1]
    while bits[-1] * 2 < line:
        bits.append(bits[-1] * 2)
    return bits


def to_place(value, d, line):
    return lax.ppermute(value, "expert", [(i, i ^ d) for i in range(line)])


def line_gather(block, line):
    got = {0: block}
    for bit in reversed(powers(line)):
        for d in list(got):
            got[d | bit] = to_place(got[d], bit, line)
    return got


def line_reduce(parts, line):
    parts = dict(enumerate(parts))
    for bit in powers(line):
        for d in sorted((d for d in parts if d & bit), reverse=True):
            moved = to_place(parts.pop(d), bit, line)
            kept = parts[d ^ bit].astype(F32) + moved.astype(F32)
            parts[d ^ bit] = kept.astype(moved.dtype)
    return parts[0]


def pick_kernel(n, cap, columns, scaled, *refs):
    slot_ref, weight_ref = refs[:2]
    blocks, pieces = refs[2 : 2 + n], refs[2 + n :]
    slots = columns * cap
    for j in range(n):
        block = blocks[j][...]
        ids = lax.broadcasted_iota(jnp.int32, (slots, block.shape[0]), 0)
        hits = [ids == slot_ref[j, k : k + 1, :] for k in range(slot_ref.shape[1])]
        pick = functools.reduce(jnp.add, [h.astype(F32) for h in hits]).astype(BF)
        rows = dot(pick, block, 1, 0)
        if scaled:
            given = functools.reduce(
                jnp.add,
                [jnp.where(h, weight_ref[j, k : k + 1, :], 0.0) for k, h in enumerate(hits)],
            )
            rows = rows * jnp.sum(given, axis=1, keepdims=True)
        rows = rows.astype(BF)
        for d in range(columns):
            pieces[d][j * cap : (j + 1) * cap, :] = rows[d * cap : (d + 1) * cap, :]


def pick_rows(slot, weight, blocks, cap, columns, scaled):
    rows, half = blocks[0].shape
    n = len(blocks)
    return pl.pallas_call(
        functools.partial(pick_kernel, n, cap, columns, scaled),
        out_shape=[jax.ShapeDtypeStruct((n * cap, half), BF)] * columns,
        in_specs=[VMEM] * (2 + n),
        out_specs=[VMEM] * columns,
        compiler_params=PARAMS,
        cost_estimate=SMALL,
        name="pick_scaled" if scaled else "pick",
    )(slot, weight, *blocks)


def stack_kernel(count, *refs):
    pieces, out = refs[:count], refs[count]
    at = 0
    for piece in pieces:
        size = piece.shape[0]
        out[at : at + size, :] = piece[...]
        at += size


def stack_rows(pieces):
    total = sum(p.shape[0] for p in pieces)
    half = pieces[0].shape[1]
    return pl.pallas_call(
        functools.partial(stack_kernel, len(pieces)),
        out_shape=jax.ShapeDtypeStruct((total, half), BF),
        in_specs=[VMEM] * len(pieces),
        out_specs=VMEM,
        compiler_params=PARAMS,
        cost_estimate=SMALL,
        name="stack",
    )(*pieces)


def join_kernel(n, cap, columns, weighted, *refs):
    slot_ref, weight_ref = refs[:2]
    pieces, rest = refs[2 : 2 + columns], refs[2 + columns :]
    held = rest[-1]
    if weighted:
        cots, parts, gates = rest[:n], rest[n : 2 * n], rest[2 * n]
    else:
        parts = rest[:n]
    slots = columns * cap
    top = slot_ref.shape[1]
    for j in range(n):
        for d in range(columns):
            held[d * cap : (d + 1) * cap, :] = pieces[d][j * cap : (j + 1) * cap, :]
        rows = held[...]
        ids = lax.broadcasted_iota(jnp.int32, (slots, slot_ref.shape[2]), 0)
        hits = [ids == slot_ref[j, k : k + 1, :] for k in range(top)]
        if weighted:
            given = functools.reduce(
                jnp.add,
                [jnp.where(h, weight_ref[j, k : k + 1, :], 0.0) for k, h in enumerate(hits)],
            )
            high = given.astype(BF)
            low = (given - high.astype(F32)).astype(BF)
            parts[j][...] = (dot(high, rows, 0, 0) + dot(low, rows, 0, 0)).astype(BF)
            meet = dot(rows, cots[j][...], 1, 1)
            for k, h in enumerate(hits):
                gates[j, k : k + 1, :] = jnp.sum(jnp.where(h, meet, 0.0), axis=0, keepdims=True)
        else:
            pick = functools.reduce(jnp.add, [h.astype(F32) for h in hits]).astype(BF)
            parts[j][...] = dot(pick, rows, 0, 0).astype(BF)


def join_rows(slot, weight, pieces, cap, cots=None):
    columns, half = len(pieces), pieces[0].shape[1]
    n, top, rows = slot.shape
    weighted = cots is not None
    outs = [jax.ShapeDtypeStruct((rows, half), BF)] * n
    if weighted:
        outs.append(jax.ShapeDtypeStruct((n, top, rows), F32))
    ins = [slot, weight] + list(pieces) + (list(cots) if weighted else [])
    out = pl.pallas_call(
        functools.partial(join_kernel, n, cap, columns, weighted),
        out_shape=outs,
        in_specs=[VMEM] * len(ins),
        out_specs=[VMEM] * len(outs),
        scratch_shapes=[pltpu.VMEM((columns * cap, half), BF)],
        compiler_params=PARAMS,
        cost_estimate=SMALL,
        name="join_weighted" if weighted else "join",
    )(*ins)
    return (list(out[:n]), out[n]) if weighted else (list(out[:n]), None)


def halves(head_ref, half):
    head = head_ref[0]
    return (
        pl.ds(pl.multiple_of(head * half, half), half),
        pl.ds(pl.multiple_of((1 - head) * half, half), half),
    )


def ahead_kernel(
    half, head_ref, mine_ref, other_ref, gate_ref, up_ref, down_ref,
    pre_gate_ref, pre_up_ref, act_ref, kept_ref, sent_ref,
):
    own, away = halves(head_ref, half)
    mine, other = mine_ref[...], other_ref[...]
    pre_gate = dot(mine, gate_ref[own, :], 1, 0) + dot(other, gate_ref[away, :], 1, 0)
    pre_up = dot(mine, up_ref[own, :], 1, 0) + dot(other, up_ref[away, :], 1, 0)
    pre_gate_ref[...] = pre_gate
    pre_up_ref[...] = pre_up
    act = (pre_gate * (1.0 / (1.0 + jnp.exp(-pre_gate))) * pre_up).astype(BF)
    act_ref[...] = act
    sent_ref[...] = dot(act, down_ref[:, away], 1, 0).astype(BF)
    kept_ref[...] = dot(act, down_ref[:, own], 1, 0).astype(BF)


def back_kernel(
    half, head_ref, mine_ref, other_ref, pre_gate_ref, pre_up_ref, gate_ref, up_ref, down_ref,
    d_gate_ref, d_up_ref, kept_ref, sent_ref,
):
    own, away = halves(head_ref, half)
    d_act = dot(mine_ref[...], down_ref[:, own], 1, 1) + dot(other_ref[...], down_ref[:, away], 1, 1)
    pre_gate, pre_up = pre_gate_ref[...], pre_up_ref[...]
    sig = 1.0 / (1.0 + jnp.exp(-pre_gate))
    d_gate = (d_act * pre_up * sig * (1.0 + pre_gate * (1.0 - sig))).astype(BF)
    d_up = (d_act * (pre_gate * sig)).astype(BF)
    d_gate_ref[...] = d_gate
    d_up_ref[...] = d_up
    for span, ref in ((away, sent_ref), (own, kept_ref)):
        ref[...] = (dot(d_gate, gate_ref[span, :], 1, 1) + dot(d_up, up_ref[span, :], 1, 1)).astype(BF)


def by_rows(kernel, head, rows_in, whole_in, outs, name):
    total, half = rows_in[0].shape
    block = min(256, total)

    def cut(width):
        return pl.BlockSpec((block, width), lambda i: (i, 0))

    return pl.pallas_call(
        functools.partial(kernel, half),
        grid=(total // block,),
        out_shape=[jax.ShapeDtypeStruct((total, width), dtype) for width, dtype in outs],
        in_specs=[SMEM]
        + [cut(v.shape[1]) for v in rows_in]
        + [pl.BlockSpec(v.shape, lambda i: (0, 0)) for v in whole_in],
        out_specs=[cut(width) for width, _ in outs],
        compiler_params=PARAMS,
        cost_estimate=SMALL,
        name=name,
    )(head, *rows_in, *whole_in)


def deal_kernel(sizes, kept_ref, came_ref, *pieces):
    at = 0
    for piece, size in zip(pieces, sizes):
        total = kept_ref[at : at + size, :].astype(F32) + came_ref[at : at + size, :].astype(F32)
        piece[...] = total.astype(BF)
        at += size


def deal_rows(kept, came, sizes):
    return pl.pallas_call(
        functools.partial(deal_kernel, sizes),
        out_shape=[jax.ShapeDtypeStruct((size, kept.shape[1]), BF) for size in sizes],
        in_specs=[VMEM, VMEM],
        out_specs=[VMEM] * len(sizes),
        compiler_params=PARAMS,
        cost_estimate=SMALL,
        name="deal",
    )(kept, came)


def together(*values):
    return lax.optimization_barrier(values)


def shards(tokens, routes, combine_weights, w_gate, w_up, w_down, cotangent):
    columns, line = lax.axis_size("path"), lax.axis_size("expert")
    column, place, head = lax.axis_index("path"), lax.axis_index("expert"), lax.axis_index("head")
    tok_rows, half = tokens.shape
    top = routes.shape[1]
    groups = columns * line
    cap = max(2, 2 * tok_rows * top // groups)
    flat = routes.reshape(-1)
    order = jnp.arange(flat.shape[0], dtype=jnp.int32)
    earlier = (flat[:, None] == flat[None, :]) & (order[:, None] < order[None, :])
    rank = jnp.sum(earlier.astype(jnp.int32), axis=0)
    position = (flat * cap + rank).astype(F32).reshape(tok_rows, top)
    about = jnp.concatenate([position.T, combine_weights.T], axis=0)

    info = jnp.stack([about] + [to_place(about, d, line) for d in range(1, line)], axis=0)
    where_to = info[:, :top].astype(jnp.int32)
    expert = where_to // cap
    slot = ((expert // line) ^ column) * cap + where_to % cap
    slot = jnp.where(expert % line == place, slot, -1)
    weight = info[:, top:]

    def exchange(pieces):
        return [pieces[0]] + [
            lax.ppermute(pieces[d], "path", [(i, i ^ d) for i in range(columns)])
            for d in range(columns - 1, 0, -1)
        ][::-1]

    near, far = slice(0, line - 1), slice(line - 1, line)

    def fetch(got, scaled):
        pieces = []
        for part in (near, far):
            blocks = [got[d] for d in range(line)[part]]
            pieces += exchange(pick_rows(slot[part], weight[part], blocks, cap, columns, scaled))
        return pieces

    tok_in = line_gather(tokens, line)
    cot_gated, _ = together(cotangent, tok_in[line - 1])
    cot_in = line_gather(cot_gated, line)

    gate_cols, up_cols, down_rows = w_gate[0], w_up[0], w_down[0]
    head_arg = head.reshape(1).astype(jnp.int32)
    hidden = gate_cols.shape[1]

    def swap(value):
        return lax.ppermute(value, "head", SWAP)

    def full(mine, other):
        first = head == 0
        return jnp.concatenate(
            [jnp.where(first, mine, other), jnp.where(first, other, mine)], axis=1
        )

    tok_mine = stack_rows(fetch(tok_in, False))
    tok_other = swap(tok_mine)
    pre_gate, pre_up, activation, out_kept, out_sent = by_rows(
        ahead_kernel,
        head_arg,
        [tok_mine, tok_other],
        [gate_cols, up_cols, down_rows],
        [(hidden, F32), (hidden, F32), (hidden, BF), (half, BF), (half, BF)],
        "ahead",
    )
    sizes = [cap * (line - 1)] * columns + [cap] * columns

    def send_home(kept, sent):
        pieces = deal_rows(kept, swap(sent), sizes)
        far_rows = exchange(pieces[columns:])
        return exchange(pieces[:columns]), far_rows

    out_near, out_far = send_home(out_kept, out_sent)
    cot_mine = stack_rows(fetch(cot_in, True))
    cot_other = swap(cot_mine)
    d_pre_gate, d_pre_up, back_kept, back_sent = by_rows(
        back_kernel,
        head_arg,
        [cot_mine, cot_other, pre_gate, pre_up],
        [gate_cols, up_cols, down_rows],
        [(hidden, BF), (hidden, BF), (half, BF), (half, BF)],
        "back",
    )
    back_near, back_far = send_home(back_kept, back_sent)

    d_pre_gate, d_pre_up, activation, _ = together(d_pre_gate, d_pre_up, activation, back_far[0])
    inbound, grad_in = full(tok_mine, tok_other), full(cot_mine, cot_other)
    grad_gate = dot(inbound, d_pre_gate, 0, 0).astype(BF)
    grad_up = dot(inbound, d_pre_up, 0, 0).astype(BF)
    grad_down = dot(activation, grad_in, 0, 0).astype(BF)

    def settle(near_rows, far_rows, cots):
        parts_far, gates_far = join_rows(
            slot[far], weight[far], far_rows, cap, None if cots is None else cots[far]
        )
        parts, gates_near = join_rows(
            slot[near], weight[near], near_rows, cap, None if cots is None else cots[near]
        )
        total = line_reduce(parts + parts_far, line)
        if cots is None:
            return total, None
        gates = [gates_near[d] for d in range(line - 1)] + [gates_far[0]]
        return total, line_reduce(gates, line)

    layer_out, local_gates = settle(out_near, out_far, [cot_in[d] for d in range(line)])
    d_tokens, _ = settle(back_near, back_far, None)
    d_gates = (local_gates + swap(local_gates)).T
    return (layer_out, d_tokens, d_gates, grad_gate[None], grad_up[None], grad_down[None])


def solution(mesh):
    rows = P(("path", "expert"), "head")
    whole = P(("path", "expert"), None)
    cols = P(("path", "expert"), None, "head")
    downs = P(("path", "expert"), "head", None)
    return jax.shard_map(
        shards,
        mesh=mesh,
        in_specs=(rows, whole, whole, cols, cols, downs, rows),
        out_specs=(rows, rows, whole, cols, cols, downs),
        check_vma=False,
    )
```

```python
import functools

import jax
import jax.numpy as jnp
from jax import lax
from jax.experimental import pallas as pl
from jax.experimental.pallas import tpu as pltpu
from jax.sharding import PartitionSpec as P

BF = jnp.bfloat16
F32 = jnp.float32
VMEM = pl.BlockSpec(memory_space=pltpu.VMEM)
SMEM = pl.BlockSpec(memory_space=pltpu.SMEM)
ANY = pl.BlockSpec(memory_space=pl.ANY)
PARAMS = pltpu.CompilerParams(vmem_limit_bytes=48 << 20)
SWAP = [(0, 1), (1, 0)]
LARGE = pl.CostEstimate(flops=400_000_000_000, bytes_accessed=40 << 20, transcendentals=0)
SMALL = pl.CostEstimate(flops=0, bytes_accessed=0, transcendentals=0)


def dot(a, b, ca, cb):
    return lax.dot_general(a, b, (((ca,), (cb,)), ((), ())), preferred_element_type=F32)


def powers(line):
    bits = [1]
    while bits[-1] * 2 < line:
        bits.append(bits[-1] * 2)
    return bits


def to_place(value, d, line):
    return lax.ppermute(value, "expert", [(i, i ^ d) for i in range(line)])


def line_gather(block, line, early=None, first=None):
    got = {0: block}
    for bit in reversed(powers(line)):
        for d in list(got):
            if d | bit in got:
                continue
            sent = early if early is not None and len(got) == 1 else got[d]
            got[d | bit] = to_place(sent, bit, line)
            if first is not None and d == 0 and bit == powers(line)[-1]:
                got[bit], _, got[1] = together(got[bit], first, to_place(block, 1, line))
    return got


def reduce_bit(parts, bit, line):
    for d in sorted((d for d in parts if d & bit), reverse=True):
        moved = to_place(parts.pop(d), bit, line)
        kept = parts[d ^ bit].astype(F32) + moved.astype(F32)
        parts[d ^ bit] = kept.astype(moved.dtype)


def pick_kernel(n, cap, columns, scaled, *refs):
    slot_ref, weight_ref = refs[:2]
    blocks, pieces = refs[2 : 2 + n], refs[2 + n :]
    slots = columns * cap
    for j in range(n):
        block = blocks[j][...]
        ids = lax.broadcasted_iota(jnp.int32, (slots, block.shape[0]), 0)
        hits = [ids == slot_ref[j, k : k + 1, :] for k in range(slot_ref.shape[1])]
        pick = functools.reduce(jnp.add, [h.astype(F32) for h in hits]).astype(BF)
        rows = dot(pick, block, 1, 0)
        if scaled:
            given = functools.reduce(
                jnp.add,
                [jnp.where(h, weight_ref[j, k : k + 1, :], 0.0) for k, h in enumerate(hits)],
            )
            rows = rows * jnp.sum(given, axis=1, keepdims=True)
        rows = rows.astype(BF)
        for d in range(columns):
            pieces[d][j * cap : (j + 1) * cap, :] = rows[d * cap : (d + 1) * cap, :]


def pick_rows(slot, weight, blocks, cap, columns, scaled, cost):
    rows, half = blocks[0].shape
    n = len(blocks)
    return list(pl.pallas_call(
        functools.partial(pick_kernel, n, cap, columns, scaled),
        out_shape=[jax.ShapeDtypeStruct((n * cap, half), BF)] * columns,
        in_specs=[VMEM] * (2 + n),
        out_specs=[VMEM] * columns,
        compiler_params=PARAMS,
        cost_estimate=cost,
        name="pick_scaled" if scaled else "pick",
    )(slot, weight, *blocks))


def stack_kernel(count, *refs):
    pieces, out = refs[:count], refs[count]
    at = 0
    for piece in pieces:
        size = piece.shape[0]
        out[at : at + size, :] = piece[...]
        at += size


def stack_rows(pieces):
    total = sum(p.shape[0] for p in pieces)
    half = pieces[0].shape[1]
    return pl.pallas_call(
        functools.partial(stack_kernel, len(pieces)),
        out_shape=jax.ShapeDtypeStruct((total, half), BF),
        in_specs=[VMEM] * len(pieces),
        out_specs=VMEM,
        compiler_params=PARAMS,
        cost_estimate=SMALL,
        name="stack",
    )(*pieces)


def join_kernel(n, cap, columns, weighted, *refs):
    slot_ref, weight_ref = refs[:2]
    pieces, rest = refs[2 : 2 + columns], refs[2 + columns :]
    held = rest[-1]
    if weighted:
        cots, parts = rest[:n], rest[n : 2 * n]
    else:
        parts = rest[:n]
    slots = columns * cap
    top = slot_ref.shape[1]
    for j in range(n):
        for d in range(columns):
            held[d * cap : (d + 1) * cap, :] = pieces[d][j * cap : (j + 1) * cap, :]
        rows = held[...]
        ids = lax.broadcasted_iota(jnp.int32, (slots, slot_ref.shape[2]), 0)
        hits = [ids == slot_ref[j, k : k + 1, :] for k in range(top)]
        if weighted:
            given = functools.reduce(
                jnp.add,
                [jnp.where(h, weight_ref[j, k : k + 1, :], 0.0) for k, h in enumerate(hits)],
            )
            high = given.astype(BF)
            low = (given - high.astype(F32)).astype(BF)
            parts[j][: high.shape[1], :] = (dot(high, rows, 0, 0) + dot(low, rows, 0, 0)).astype(BF)
            meet = dot(rows, cots[j][...], 1, 1)
            width = meet.shape[1]
            for k, h in enumerate(hits):
                gate = jnp.sum(jnp.where(h, meet, 0.0), axis=0, keepdims=True)
                gate_high = gate.astype(BF)
                gate_low = (gate - gate_high.astype(F32)).astype(BF)
                for half_at, value in ((0, gate_high), (top, gate_low)):
                    at = (half_at + k) * width
                    parts[j][width : width + 16, at : at + width] = jnp.broadcast_to(value, (16, width))
        else:
            pick = functools.reduce(jnp.add, [h.astype(F32) for h in hits]).astype(BF)
            parts[j][...] = dot(pick, rows, 0, 0).astype(BF)


def join_rows(slot, weight, pieces, cap, cots=None):
    columns, half = len(pieces), pieces[0].shape[1]
    n, top, rows = slot.shape
    weighted = cots is not None
    outs = [jax.ShapeDtypeStruct((rows + (16 if weighted else 0), half), BF)] * n
    ins = [slot, weight] + list(pieces) + (list(cots) if weighted else [])
    out = pl.pallas_call(
        functools.partial(join_kernel, n, cap, columns, weighted),
        out_shape=outs,
        in_specs=[VMEM] * len(ins),
        out_specs=[VMEM] * len(outs),
        scratch_shapes=[pltpu.VMEM((columns * cap, half), BF)],
        compiler_params=PARAMS,
        cost_estimate=LARGE,
        name="join_weighted" if weighted else "join",
    )(*ins)
    return list(out)


def halves(head_ref, half):
    head = head_ref[0]
    return (
        pl.ds(pl.multiple_of(head * half, half), half),
        pl.ds(pl.multiple_of((1 - head) * half, half), half),
    )


def ahead_kernel(
    half, head_ref, mine_ref, other_ref, gate_ref, up_ref, down_ref,
    pre_gate_ref, pre_up_ref, act_ref, kept_ref, sent_ref,
):
    own, away = halves(head_ref, half)
    mine, other = mine_ref[...], other_ref[...]
    pre_gate = dot(mine, gate_ref[own, :], 1, 0) + dot(other, gate_ref[away, :], 1, 0)
    pre_up = dot(mine, up_ref[own, :], 1, 0) + dot(other, up_ref[away, :], 1, 0)
    pre_gate_ref[...] = pre_gate
    pre_up_ref[...] = pre_up
    act = (pre_gate * (1.0 / (1.0 + jnp.exp(-pre_gate))) * pre_up).astype(BF)
    act_ref[...] = act
    sent_ref[...] = dot(act, down_ref[:, away], 1, 0).astype(BF)
    kept_ref[...] = dot(act, down_ref[:, own], 1, 0).astype(BF)


def back_kernel(
    half, head_ref, mine_ref, other_ref, pre_gate_ref, pre_up_ref, gate_ref, up_ref, down_ref,
    d_gate_ref, d_up_ref, kept_ref, sent_ref,
):
    own, away = halves(head_ref, half)
    d_act = dot(mine_ref[...], down_ref[:, own], 1, 1) + dot(other_ref[...], down_ref[:, away], 1, 1)
    pre_gate, pre_up = pre_gate_ref[...], pre_up_ref[...]
    sig = 1.0 / (1.0 + jnp.exp(-pre_gate))
    d_gate = (d_act * pre_up * sig * (1.0 + pre_gate * (1.0 - sig))).astype(BF)
    d_up = (d_act * (pre_gate * sig)).astype(BF)
    d_gate_ref[...] = d_gate
    d_up_ref[...] = d_up
    for span, ref in ((away, sent_ref), (own, kept_ref)):
        ref[...] = (dot(d_gate, gate_ref[span, :], 1, 1) + dot(d_up, up_ref[span, :], 1, 1)).astype(BF)


def by_rows(kernel, head, rows_in, whole_in, outs, name):
    total, half = rows_in[0].shape
    block = min(256, total)

    def cut(width):
        return pl.BlockSpec((block, width), lambda i: (i, 0))

    return pl.pallas_call(
        functools.partial(kernel, half),
        grid=(total // block,),
        out_shape=[jax.ShapeDtypeStruct((total, width), dtype) for width, dtype in outs],
        in_specs=[SMEM]
        + [cut(v.shape[1]) for v in rows_in]
        + [pl.BlockSpec(v.shape, lambda i: (0, 0)) for v in whole_in],
        out_specs=[cut(width) for width, _ in outs],
        compiler_params=PARAMS,
        cost_estimate=LARGE,
        name=name,
    )(head, *rows_in, *whole_in)


def deal_kernel(sizes, kept_ref, came_ref, *pieces):
    at = 0
    for piece, size in zip(pieces, sizes):
        total = kept_ref[at : at + size, :].astype(F32) + came_ref[at : at + size, :].astype(F32)
        piece[...] = total.astype(BF)
        at += size


def deal_rows(kept, came, sizes):
    return pl.pallas_call(
        functools.partial(deal_kernel, sizes),
        out_shape=[jax.ShapeDtypeStruct((size, kept.shape[1]), BF) for size in sizes],
        in_specs=[VMEM, VMEM],
        out_specs=[VMEM] * len(sizes),
        compiler_params=PARAMS,
        cost_estimate=SMALL,
        name="deal",
    )(kept, came)


def together(*values):
    return lax.optimization_barrier(values)


def shards(tokens, routes, combine_weights, w_gate, w_up, w_down, cotangent):
    columns, line = lax.axis_size("path"), lax.axis_size("expert")
    column, place, head = lax.axis_index("path"), lax.axis_index("expert"), lax.axis_index("head")
    tok_rows, half = tokens.shape
    top = routes.shape[1]
    groups = columns * line
    cap = max(2, 2 * tok_rows * top // groups)
    def after(value, *others):
        return together(value, *others)[0]

    flat = routes.reshape(-1)
    order = jnp.arange(flat.shape[0], dtype=jnp.int32)
    earlier = (flat[:, None] == flat[None, :]) & (order[:, None] < order[None, :])
    rank = jnp.sum(earlier.astype(jnp.int32), axis=0)
    position = (flat * cap + rank).astype(F32).reshape(tok_rows, top)
    about = jnp.concatenate([position.T, combine_weights.T], axis=0)

    def exchange(pieces):
        return [pieces[0]] + [
            lax.ppermute(pieces[d], "path", [(i, i ^ d) for i in range(columns)])
            for d in range(columns - 1, 0, -1)
        ][::-1]

    near, far = slice(0, line - 1), slice(line - 1, line)

    every = slice(0, line)

    def pick_group(got, part, scaled, cost=SMALL):
        blocks = [got[d] for d in range(line)[part]]
        return pick_rows(slot[part], weight[part], blocks, cap, columns, scaled, cost)

    first_bit = powers(line)[-1]
    info = jnp.stack([about] + [to_place(about, d, line) for d in range(1, line)], axis=0)
    where_to = info[:, :top].astype(jnp.int32)
    expert = where_to // cap
    slot = ((expert // line) ^ column) * cap + where_to % cap
    slot = jnp.where(expert % line == place, slot, -1)
    weight = info[:, top:]
    tok_in = line_gather(tokens, line, first=info)

    cot_far = after(cotangent, tok_in[first_bit])
    cot_near = after(cotangent, tok_in[line - 1])
    cot_in = line_gather(cot_near, line, cot_far)

    gate_cols, up_cols, down_rows = w_gate[0], w_up[0], w_down[0]
    head_arg = head.reshape(1).astype(jnp.int32)
    hidden = gate_cols.shape[1]

    def swap(value):
        return lax.ppermute(value, "head", SWAP)

    def full(mine, other):
        first = head == 0
        return jnp.concatenate(
            [jnp.where(first, mine, other), jnp.where(first, other, mine)], axis=1
        )

    tok_near = exchange(pick_group(tok_in, near, False))
    tok_in[line - 1] = after(tok_in[line - 1], *tok_near[1:])
    tok_far = exchange(pick_group(tok_in, far, False))
    tok_far[-1] = after(tok_far[-1], cot_in[first_bit], cot_in[1])
    tok_mine = stack_rows([p for pair in zip(tok_near, tok_far) for p in pair])
    cot_in[0] = after(cot_in[0], tok_mine)
    cot_near_rows = pick_group(cot_in, near, True)
    tok_other = after(swap(tok_mine), cot_near_rows[0])
    pre_gate, pre_up, activation, out_kept, out_sent = by_rows(
        ahead_kernel,
        head_arg,
        [tok_mine, tok_other],
        [gate_cols, up_cols, down_rows],
        [(hidden, F32), (hidden, F32), (hidden, BF), (half, BF), (half, BF)],
        "ahead",
    )
    cot_near_in = exchange(cot_near_rows)
    cot_in[line - 1] = after(cot_in[line - 1], out_sent, *cot_near_in[1:])
    cot_far_rows = pick_group(cot_in, far, True, LARGE)
    out_came = after(swap(out_sent), cot_far_rows[0])
    out_pieces = deal_rows(out_kept, out_came, [cap * (line - 1), cap] * columns)
    cot_far_in = exchange(cot_far_rows)
    out_far = exchange(out_pieces[1::2])
    cot_mine = stack_rows([p for pair in zip(cot_near_in, cot_far_in) for p in pair])
    cots = [cot_in[d] for d in range(line)]
    out_far[-1] = after(out_far[-1], cot_mine)
    out_parts_far = join_rows(slot[far], weight[far], out_far, cap, cots[far])
    out_near = exchange(list(together(*out_pieces[::2], cot_mine)[:-1]))
    cot_other = after(swap(cot_mine), out_parts_far[0])
    d_pre_gate, d_pre_up, back_kept, back_sent = by_rows(
        back_kernel,
        head_arg,
        [cot_mine, cot_other, pre_gate, pre_up],
        [gate_cols, up_cols, down_rows],
        [(hidden, BF), (hidden, BF), (half, BF), (half, BF)],
        "back",
    )
    out_near[-1] = after(out_near[-1], back_sent)
    out_parts = join_rows(slot[near], weight[near], out_near, cap, cots[near]) + out_parts_far
    back_came = after(swap(back_sent), out_parts[0])
    first, last = slice(0, line - 2), slice(line - 2, line)
    back_pieces = deal_rows(back_kept, back_came, [cap * (line - 2), cap * 2] * columns)
    back_last = exchange(back_pieces[1::2])
    out_parts[0] = after(out_parts[0], *back_pieces)
    out_sums = dict(enumerate(out_parts))
    reduce_bit(out_sums, 1, line)
    back_last[-1] = after(back_last[-1], *out_sums.values())
    back_parts_last = join_rows(slot[last], weight[last], back_last, cap)
    back_first = exchange(
        [back_pieces[0]] + list(together(*back_pieces[2::2], *back_last[1:])[: columns - 1])
    )
    moved = to_place(back_parts_last[1], 1, line)

    d_pre_gate, d_pre_up, tok_mine, tok_other, _ = together(
        d_pre_gate, d_pre_up, tok_mine, tok_other, back_parts_last[0]
    )
    inbound = full(tok_mine, tok_other)
    grad_gate = dot(inbound, d_pre_gate, 0, 0).astype(BF)
    grad_up = dot(inbound, d_pre_up, 0, 0).astype(BF)

    moved = after(moved, grad_gate, grad_up)
    back_pair = (back_parts_last[0].astype(F32) + moved.astype(F32)).astype(BF)
    activation, cot_mine, cot_other, _ = together(activation, cot_mine, cot_other, back_pair)
    grad_down = dot(activation, full(cot_mine, cot_other), 0, 0).astype(BF)

    out_sums[0] = after(out_sums[0], back_pair)
    for bit in powers(line)[1:]:
        reduce_bit(out_sums, bit, line)
    out_total = out_sums[0]
    back_first[-1] = after(back_first[-1], back_pair, out_total)
    back_sums = dict(enumerate(join_rows(slot[first], weight[first], back_first, cap) + [back_pair]))
    for bit in powers(line):
        reduce_bit(back_sums, bit, line)
    d_tokens = back_sums[0]
    layer_out = out_total[:tok_rows]
    gate_terms = out_total[tok_rows, : 2 * top * tok_rows].astype(F32).reshape(2, top, tok_rows)
    local_gates = gate_terms[0] + gate_terms[1]
    d_gates = (local_gates + swap(local_gates)).T
    return (layer_out, d_tokens, d_gates, grad_gate[None], grad_up[None], grad_down[None])


def solution(mesh):
    rows = P(("path", "expert"), "head")
    whole = P(("path", "expert"), None)
    cols = P(("path", "expert"), None, "head")
    downs = P(("path", "expert"), "head", None)
    return jax.shard_map(
        shards,
        mesh=mesh,
        in_specs=(rows, whole, whole, cols, cols, downs, rows),
        out_specs=(rows, rows, whole, cols, cols, downs),
        check_vma=False,
    )
```

```python
import functools

import jax
import jax.numpy as jnp
from jax import lax
from jax.experimental import pallas as pl
from jax.experimental.pallas import tpu as pltpu
from jax.sharding import PartitionSpec as P

BF = jnp.bfloat16
F32 = jnp.float32
VMEM = pl.BlockSpec(memory_space=pltpu.VMEM)
SMEM = pl.BlockSpec(memory_space=pltpu.SMEM)
ANY = pl.BlockSpec(memory_space=pl.ANY)
PARAMS = pltpu.CompilerParams(vmem_limit_bytes=48 << 20)
SWAP = [(0, 1), (1, 0)]
LARGE = pl.CostEstimate(flops=400_000_000_000, bytes_accessed=40 << 20, transcendentals=0)
SMALL = pl.CostEstimate(flops=0, bytes_accessed=0, transcendentals=0)


def dot(a, b, ca, cb):
    return lax.dot_general(a, b, (((ca,), (cb,)), ((), ())), preferred_element_type=F32)


def powers(line):
    bits = [1]
    while bits[-1] * 2 < line:
        bits.append(bits[-1] * 2)
    return bits


def to_place(value, d, line):
    return lax.ppermute(value, "expert", [(i, i ^ d) for i in range(line)])


def line_gather(block, line, early=None, first=None):
    got = {0: block}
    for bit in reversed(powers(line)):
        for d in list(got):
            if d | bit in got:
                continue
            sent = early if early is not None and len(got) == 1 else got[d]
            got[d | bit] = to_place(sent, bit, line)
            if first is not None and d == 0 and bit == powers(line)[-1]:
                got[bit], _, got[1] = together(got[bit], first, to_place(block, 1, line))
    return got


def reduce_bit(parts, bit, line):
    for d in sorted((d for d in parts if d & bit), reverse=True):
        moved = to_place(parts.pop(d), bit, line)
        kept = parts[d ^ bit].astype(F32) + moved.astype(F32)
        parts[d ^ bit] = kept.astype(moved.dtype)


def pick_kernel(n, cap, columns, scaled, *refs):
    slot_ref, weight_ref = refs[:2]
    blocks, pieces = refs[2 : 2 + n], refs[2 + n :]
    slots = columns * cap
    for j in range(n):
        block = blocks[j][...]
        ids = lax.broadcasted_iota(jnp.int32, (slots, block.shape[0]), 0)
        hits = [ids == slot_ref[j, k : k + 1, :] for k in range(slot_ref.shape[1])]
        pick = functools.reduce(jnp.add, [h.astype(F32) for h in hits]).astype(BF)
        rows = dot(pick, block, 1, 0)
        if scaled:
            given = functools.reduce(
                jnp.add,
                [jnp.where(h, weight_ref[j, k : k + 1, :], 0.0) for k, h in enumerate(hits)],
            )
            rows = rows * jnp.sum(given, axis=1, keepdims=True)
        rows = rows.astype(BF)
        for d in range(columns):
            pieces[d][j * cap : (j + 1) * cap, :] = rows[d * cap : (d + 1) * cap, :]


def pick_rows(slot, weight, blocks, cap, columns, scaled, cost):
    rows, half = blocks[0].shape
    n = len(blocks)
    return list(pl.pallas_call(
        functools.partial(pick_kernel, n, cap, columns, scaled),
        out_shape=[jax.ShapeDtypeStruct((n * cap, half), BF)] * columns,
        in_specs=[VMEM] * (2 + n),
        out_specs=[VMEM] * columns,
        compiler_params=PARAMS,
        cost_estimate=cost,
        name="pick_scaled" if scaled else "pick",
    )(slot, weight, *blocks))


def stack_kernel(count, *refs):
    pieces, out = refs[:count], refs[count]
    at = 0
    for piece in pieces:
        size = piece.shape[0]
        out[at : at + size, :] = piece[...]
        at += size


def stack_rows(pieces):
    total = sum(p.shape[0] for p in pieces)
    half = pieces[0].shape[1]
    return pl.pallas_call(
        functools.partial(stack_kernel, len(pieces)),
        out_shape=jax.ShapeDtypeStruct((total, half), BF),
        in_specs=[VMEM] * len(pieces),
        out_specs=VMEM,
        compiler_params=PARAMS,
        cost_estimate=SMALL,
        name="stack",
    )(*pieces)


def join_kernel(n, cap, columns, weighted, *refs):
    slot_ref, weight_ref = refs[:2]
    pieces, rest = refs[2 : 2 + columns], refs[2 + columns :]
    held = rest[-1]
    if weighted:
        cots, parts = rest[:n], rest[n : 2 * n]
    else:
        parts = rest[:n]
    slots = columns * cap
    top = slot_ref.shape[1]
    for j in range(n):
        for d in range(columns):
            held[d * cap : (d + 1) * cap, :] = pieces[d][j * cap : (j + 1) * cap, :]
        rows = held[...]
        ids = lax.broadcasted_iota(jnp.int32, (slots, slot_ref.shape[2]), 0)
        hits = [ids == slot_ref[j, k : k + 1, :] for k in range(top)]
        if weighted:
            given = functools.reduce(
                jnp.add,
                [jnp.where(h, weight_ref[j, k : k + 1, :], 0.0) for k, h in enumerate(hits)],
            )
            high = given.astype(BF)
            low = (given - high.astype(F32)).astype(BF)
            parts[j][: high.shape[1], :] = (dot(high, rows, 0, 0) + dot(low, rows, 0, 0)).astype(BF)
            meet = dot(rows, cots[j][...], 1, 1)
            width = meet.shape[1]
            for k, h in enumerate(hits):
                gate = jnp.sum(jnp.where(h, meet, 0.0), axis=0, keepdims=True)
                gate_high = gate.astype(BF)
                gate_low = (gate - gate_high.astype(F32)).astype(BF)
                for half_at, value in ((0, gate_high), (top, gate_low)):
                    at = (half_at + k) * width
                    parts[j][width : width + 16, at : at + width] = jnp.broadcast_to(value, (16, width))
        else:
            pick = functools.reduce(jnp.add, [h.astype(F32) for h in hits]).astype(BF)
            parts[j][...] = dot(pick, rows, 0, 0).astype(BF)


def join_rows(slot, weight, pieces, cap, cots=None):
    columns, half = len(pieces), pieces[0].shape[1]
    n, top, rows = slot.shape
    weighted = cots is not None
    outs = [jax.ShapeDtypeStruct((rows + (16 if weighted else 0), half), BF)] * n
    ins = [slot, weight] + list(pieces) + (list(cots) if weighted else [])
    out = pl.pallas_call(
        functools.partial(join_kernel, n, cap, columns, weighted),
        out_shape=outs,
        in_specs=[VMEM] * len(ins),
        out_specs=[VMEM] * len(outs),
        scratch_shapes=[pltpu.VMEM((columns * cap, half), BF)],
        compiler_params=PARAMS,
        cost_estimate=LARGE,
        name="join_weighted" if weighted else "join",
    )(*ins)
    return list(out)


def halves(head_ref, half):
    head = head_ref[0]
    return (
        pl.ds(pl.multiple_of(head * half, half), half),
        pl.ds(pl.multiple_of((1 - head) * half, half), half),
    )


def ahead_kernel(
    half, head_ref, mine_ref, other_ref, gate_ref, up_ref, down_ref,
    pre_gate_ref, pre_up_ref, act_ref, kept_ref, sent_ref,
):
    own, away = halves(head_ref, half)
    mine, other = mine_ref[...], other_ref[...]
    pre_gate = dot(mine, gate_ref[own, :], 1, 0) + dot(other, gate_ref[away, :], 1, 0)
    pre_up = dot(mine, up_ref[own, :], 1, 0) + dot(other, up_ref[away, :], 1, 0)
    pre_gate_ref[...] = pre_gate
    pre_up_ref[...] = pre_up
    act = (pre_gate * (1.0 / (1.0 + jnp.exp(-pre_gate))) * pre_up).astype(BF)
    act_ref[...] = act
    sent_ref[...] = dot(act, down_ref[:, away], 1, 0).astype(BF)
    kept_ref[...] = dot(act, down_ref[:, own], 1, 0).astype(BF)


def back_kernel(
    half, head_ref, mine_ref, other_ref, pre_gate_ref, pre_up_ref, gate_ref, up_ref, down_ref,
    d_gate_ref, d_up_ref, kept_ref, sent_ref,
):
    own, away = halves(head_ref, half)
    d_act = dot(mine_ref[...], down_ref[:, own], 1, 1) + dot(other_ref[...], down_ref[:, away], 1, 1)
    pre_gate, pre_up = pre_gate_ref[...], pre_up_ref[...]
    sig = 1.0 / (1.0 + jnp.exp(-pre_gate))
    d_gate = (d_act * pre_up * sig * (1.0 + pre_gate * (1.0 - sig))).astype(BF)
    d_up = (d_act * (pre_gate * sig)).astype(BF)
    d_gate_ref[...] = d_gate
    d_up_ref[...] = d_up
    for span, ref in ((away, sent_ref), (own, kept_ref)):
        ref[...] = (dot(d_gate, gate_ref[span, :], 1, 1) + dot(d_up, up_ref[span, :], 1, 1)).astype(BF)


def by_rows(kernel, head, rows_in, whole_in, outs, name):
    total, half = rows_in[0].shape
    block = min(256, total)

    def cut(width):
        return pl.BlockSpec((block, width), lambda i: (i, 0))

    return pl.pallas_call(
        functools.partial(kernel, half),
        grid=(total // block,),
        out_shape=[jax.ShapeDtypeStruct((total, width), dtype) for width, dtype in outs],
        in_specs=[SMEM]
        + [cut(v.shape[1]) for v in rows_in]
        + [pl.BlockSpec(v.shape, lambda i: (0, 0)) for v in whole_in],
        out_specs=[cut(width) for width, _ in outs],
        compiler_params=PARAMS,
        cost_estimate=LARGE,
        name=name,
    )(head, *rows_in, *whole_in)


def deal_kernel(sizes, kept_ref, came_ref, *pieces):
    at = 0
    for piece, size in zip(pieces, sizes):
        total = kept_ref[at : at + size, :].astype(F32) + came_ref[at : at + size, :].astype(F32)
        piece[...] = total.astype(BF)
        at += size


def deal_rows(kept, came, sizes):
    return pl.pallas_call(
        functools.partial(deal_kernel, sizes),
        out_shape=[jax.ShapeDtypeStruct((size, kept.shape[1]), BF) for size in sizes],
        in_specs=[VMEM, VMEM],
        out_specs=[VMEM] * len(sizes),
        compiler_params=PARAMS,
        cost_estimate=SMALL,
        name="deal",
    )(kept, came)


def together(*values):
    return lax.optimization_barrier(values)


def shards(tokens, routes, combine_weights, w_gate, w_up, w_down, cotangent):
    columns, line = lax.axis_size("path"), lax.axis_size("expert")
    column, place, head = lax.axis_index("path"), lax.axis_index("expert"), lax.axis_index("head")
    tok_rows, half = tokens.shape
    top = routes.shape[1]
    groups = columns * line
    cap = max(2, 2 * tok_rows * top // groups)
    def after(value, *others):
        return together(value, *others)[0]

    flat = routes.reshape(-1)
    order = jnp.arange(flat.shape[0], dtype=jnp.int32)
    earlier = (flat[:, None] == flat[None, :]) & (order[:, None] < order[None, :])
    rank = jnp.sum(earlier.astype(jnp.int32), axis=0)
    position = (flat * cap + rank).astype(F32).reshape(tok_rows, top)
    about = jnp.concatenate([position.T, combine_weights.T], axis=0)

    def exchange(pieces):
        return [pieces[0]] + [
            lax.ppermute(pieces[d], "path", [(i, i ^ d) for i in range(columns)])
            for d in range(columns - 1, 0, -1)
        ][::-1]

    near, far = slice(0, line - 1), slice(line - 1, line)

    every = slice(0, line)

    def pick_group(got, part, scaled, cost=SMALL):
        blocks = [got[d] for d in range(line)[part]]
        return pick_rows(slot[part], weight[part], blocks, cap, columns, scaled, cost)

    first_bit = powers(line)[-1]
    info = jnp.stack([about] + [to_place(about, d, line) for d in range(1, line)], axis=0)
    where_to = info[:, :top].astype(jnp.int32)
    expert = where_to // cap
    slot = ((expert // line) ^ column) * cap + where_to % cap
    slot = jnp.where(expert % line == place, slot, -1)
    weight = info[:, top:]
    tok_in = line_gather(tokens, line, first=info)

    cot_far = after(cotangent, tok_in[first_bit])
    cot_near = after(cotangent, tok_in[line - 1])
    cot_in = line_gather(cot_near, line, cot_far)

    gate_cols, up_cols, down_rows = w_gate[0], w_up[0], w_down[0]
    head_arg = head.reshape(1).astype(jnp.int32)
    hidden = gate_cols.shape[1]

    def swap(value):
        return lax.ppermute(value, "head", SWAP)

    def full(mine, other):
        first = head == 0
        return jnp.concatenate(
            [jnp.where(first, mine, other), jnp.where(first, other, mine)], axis=1
        )

    tok_near = exchange(pick_group(tok_in, near, False))
    tok_in[line - 1] = after(tok_in[line - 1], *tok_near[1:])
    tok_far = exchange(pick_group(tok_in, far, False))
    tok_far[-1] = after(tok_far[-1], cot_in[first_bit], cot_in[1])
    tok_mine = stack_rows([p for pair in zip(tok_near, tok_far) for p in pair])
    cot_in[0] = after(cot_in[0], tok_mine)
    cot_near_rows = pick_group(cot_in, near, True)
    tok_other = after(swap(tok_mine), cot_near_rows[0])
    pre_gate, pre_up, activation, out_kept, out_sent = by_rows(
        ahead_kernel,
        head_arg,
        [tok_mine, tok_other],
        [gate_cols, up_cols, down_rows],
        [(hidden, F32), (hidden, F32), (hidden, BF), (half, BF), (half, BF)],
        "ahead",
    )
    cot_near_in = exchange(cot_near_rows)
    cot_in[line - 1] = after(cot_in[line - 1], out_sent)
    cot_far_rows = pick_group(cot_in, far, True, LARGE)
    out_came = after(swap(out_sent), cot_far_rows[0])
    out_pieces = deal_rows(out_kept, out_came, [cap * (line - 1), cap] * columns)
    cot_far_in = exchange(cot_far_rows)
    out_far = exchange(out_pieces[1::2])
    cot_mine = stack_rows([p for pair in zip(cot_near_in, cot_far_in) for p in pair])
    cots = [cot_in[d] for d in range(line)]
    out_far[-1] = after(out_far[-1], cot_mine)
    out_parts_far = join_rows(slot[far], weight[far], out_far, cap, cots[far])
    out_near = exchange(list(together(*out_pieces[::2], cot_mine)[:-1]))
    cot_other = after(swap(cot_mine), out_parts_far[0])
    d_pre_gate, d_pre_up, back_kept, back_sent = by_rows(
        back_kernel,
        head_arg,
        [cot_mine, cot_other, pre_gate, pre_up],
        [gate_cols, up_cols, down_rows],
        [(hidden, BF), (hidden, BF), (half, BF), (half, BF)],
        "back",
    )
    out_near[-1] = after(out_near[-1], back_sent)
    out_parts = join_rows(slot[near], weight[near], out_near, cap, cots[near]) + out_parts_far
    back_came = after(swap(back_sent), out_parts[0])
    first, last = slice(0, line - 2), slice(line - 2, line)
    back_pieces = deal_rows(back_kept, back_came, [cap * (line - 2), cap * 2] * columns)
    back_last = exchange(back_pieces[1::2])
    out_parts[0] = after(out_parts[0], *back_pieces)
    out_parts[line - 2] = after(out_parts[line - 2], *back_pieces)
    out_sums = dict(enumerate(out_parts))
    reduce_bit(out_sums, 1, line)
    back_last[-1] = after(back_last[-1], *out_sums.values())
    back_parts_last = join_rows(slot[last], weight[last], back_last, cap)
    back_first = exchange(
        [back_pieces[0]] + list(together(*back_pieces[2::2], *back_last[1:])[: columns - 1])
    )
    moved = to_place(back_parts_last[1], 1, line)

    d_pre_gate, d_pre_up, tok_mine, tok_other, _ = together(
        d_pre_gate, d_pre_up, tok_mine, tok_other, back_parts_last[0]
    )
    inbound = full(tok_mine, tok_other)
    grad_gate = dot(inbound, d_pre_gate, 0, 0).astype(BF)
    grad_up = dot(inbound, d_pre_up, 0, 0).astype(BF)

    back_first[-1] = after(back_first[-1], grad_gate, grad_up)
    back_parts = join_rows(slot[first], weight[first], back_first, cap)
    moved = after(moved, back_parts[0])
    back_pair = (back_parts_last[0].astype(F32) + moved.astype(F32)).astype(BF)
    activation, cot_mine, cot_other, _ = together(activation, cot_mine, cot_other, back_pair)
    grad_down = dot(activation, full(cot_mine, cot_other), 0, 0).astype(BF)

    out_sums[0] = after(out_sums[0], back_pair)
    for bit in powers(line)[1:]:
        reduce_bit(out_sums, bit, line)
    out_total = out_sums[0]
    back_parts[0] = after(back_parts[0], out_total)
    back_sums = dict(enumerate(back_parts + [back_pair]))
    for bit in powers(line):
        reduce_bit(back_sums, bit, line)
    d_tokens = back_sums[0]
    layer_out = out_total[:tok_rows]
    gate_terms = out_total[tok_rows, : 2 * top * tok_rows].astype(F32).reshape(2, top, tok_rows)
    local_gates = gate_terms[0] + gate_terms[1]
    d_gates = (local_gates + swap(local_gates)).T
    return (layer_out, d_tokens, d_gates, grad_gate[None], grad_up[None], grad_down[None])


def solution(mesh):
    rows = P(("path", "expert"), "head")
    whole = P(("path", "expert"), None)
    cols = P(("path", "expert"), None, "head")
    downs = P(("path", "expert"), "head", None)
    return jax.shard_map(
        shards,
        mesh=mesh,
        in_specs=(rows, whole, whole, cols, cols, downs, rows),
        out_specs=(rows, rows, whole, cols, cols, downs),
        check_vma=False,
    )
```

```python
import functools

import jax
import jax.numpy as jnp
from jax import lax
from jax.experimental import pallas as pl
from jax.experimental.pallas import tpu as pltpu
from jax.sharding import PartitionSpec as P

BF = jnp.bfloat16
F32 = jnp.float32
VMEM = pl.BlockSpec(memory_space=pltpu.VMEM)
SMEM = pl.BlockSpec(memory_space=pltpu.SMEM)
ANY = pl.BlockSpec(memory_space=pl.ANY)
PARAMS = pltpu.CompilerParams(vmem_limit_bytes=48 << 20)
SWAP = [(0, 1), (1, 0)]
LARGE = pl.CostEstimate(flops=400_000_000_000, bytes_accessed=40 << 20, transcendentals=0)
SMALL = pl.CostEstimate(flops=0, bytes_accessed=0, transcendentals=0)


def dot(a, b, ca, cb):
    return lax.dot_general(a, b, (((ca,), (cb,)), ((), ())), preferred_element_type=F32)


def powers(line):
    bits = [1]
    while bits[-1] * 2 < line:
        bits.append(bits[-1] * 2)
    return bits


def to_place(value, d, line):
    return lax.ppermute(value, "expert", [(i, i ^ d) for i in range(line)])


def line_gather(block, line, early=None, first=None):
    got = {0: block}
    for bit in reversed(powers(line)):
        for d in list(got):
            if d | bit in got:
                continue
            sent = early if early is not None and len(got) == 1 else got[d]
            got[d | bit] = to_place(sent, bit, line)
            if first is not None and d == 0 and bit == powers(line)[-1]:
                got[bit], _, got[1] = together(got[bit], first, to_place(block, 1, line))
    return got


def reduce_bit(parts, bit, line):
    for d in sorted((d for d in parts if d & bit), reverse=True):
        moved = to_place(parts.pop(d), bit, line)
        kept = parts[d ^ bit].astype(F32) + moved.astype(F32)
        parts[d ^ bit] = kept.astype(moved.dtype)


def pick_kernel(n, cap, columns, scaled, *refs):
    slot_ref, weight_ref = refs[:2]
    blocks, pieces = refs[2 : 2 + n], refs[2 + n :]
    slots = columns * cap
    for j in range(n):
        block = blocks[j][...]
        ids = lax.broadcasted_iota(jnp.int32, (slots, block.shape[0]), 0)
        hits = [ids == slot_ref[j, k : k + 1, :] for k in range(slot_ref.shape[1])]
        pick = functools.reduce(jnp.add, [h.astype(F32) for h in hits]).astype(BF)
        rows = dot(pick, block, 1, 0)
        if scaled:
            given = functools.reduce(
                jnp.add,
                [jnp.where(h, weight_ref[j, k : k + 1, :], 0.0) for k, h in enumerate(hits)],
            )
            rows = rows * jnp.sum(given, axis=1, keepdims=True)
        rows = rows.astype(BF)
        for d in range(columns):
            pieces[d][j * cap : (j + 1) * cap, :] = rows[d * cap : (d + 1) * cap, :]


def pick_rows(slot, weight, blocks, cap, columns, scaled, cost):
    rows, half = blocks[0].shape
    n = len(blocks)
    return list(pl.pallas_call(
        functools.partial(pick_kernel, n, cap, columns, scaled),
        out_shape=[jax.ShapeDtypeStruct((n * cap, half), BF)] * columns,
        in_specs=[VMEM] * (2 + n),
        out_specs=[VMEM] * columns,
        compiler_params=PARAMS,
        cost_estimate=cost,
        name="pick_scaled" if scaled else "pick",
    )(slot, weight, *blocks))


def stack_kernel(count, *refs):
    pieces, out = refs[:count], refs[count]
    at = 0
    for piece in pieces:
        size = piece.shape[0]
        out[at : at + size, :] = piece[...]
        at += size


def stack_rows(pieces):
    total = sum(p.shape[0] for p in pieces)
    half = pieces[0].shape[1]
    return pl.pallas_call(
        functools.partial(stack_kernel, len(pieces)),
        out_shape=jax.ShapeDtypeStruct((total, half), BF),
        in_specs=[VMEM] * len(pieces),
        out_specs=VMEM,
        compiler_params=PARAMS,
        cost_estimate=SMALL,
        name="stack",
    )(*pieces)


def join_kernel(n, cap, columns, weighted, cuts, *refs):
    slot_ref, weight_ref = refs[:2]
    pieces, rest = refs[2 : 2 + columns], refs[2 + columns :]
    held = rest[-1]
    if weighted:
        cots, parts = rest[:n], rest[n : 2 * n]
    else:
        parts = rest[: n * cuts]
    slots = columns * cap
    top = slot_ref.shape[1]
    for j in range(n):
        for d in range(columns):
            held[d * cap : (d + 1) * cap, :] = pieces[d][j * cap : (j + 1) * cap, :]
        rows = held[...]
        ids = lax.broadcasted_iota(jnp.int32, (slots, slot_ref.shape[2]), 0)
        hits = [ids == slot_ref[j, k : k + 1, :] for k in range(top)]
        if weighted:
            given = functools.reduce(
                jnp.add,
                [jnp.where(h, weight_ref[j, k : k + 1, :], 0.0) for k, h in enumerate(hits)],
            )
            high = given.astype(BF)
            low = (given - high.astype(F32)).astype(BF)
            parts[j][: high.shape[1], :] = (dot(high, rows, 0, 0) + dot(low, rows, 0, 0)).astype(BF)
            meet = dot(rows, cots[j][...], 1, 1)
            width = meet.shape[1]
            for k, h in enumerate(hits):
                gate = jnp.sum(jnp.where(h, meet, 0.0), axis=0, keepdims=True)
                gate_high = gate.astype(BF)
                gate_low = (gate - gate_high.astype(F32)).astype(BF)
                for half_at, value in ((0, gate_high), (top, gate_low)):
                    at = (half_at + k) * width
                    parts[j][width : width + 16, at : at + width] = jnp.broadcast_to(value, (16, width))
        else:
            pick = functools.reduce(jnp.add, [h.astype(F32) for h in hits]).astype(BF)
            total = dot(pick, rows, 0, 0).astype(BF)
            width = total.shape[1] // cuts
            for s in range(cuts):
                parts[j * cuts + s][...] = total[:, s * width : (s + 1) * width]


def join_rows(slot, weight, pieces, cap, cots=None, cuts=1):
    columns, half = len(pieces), pieces[0].shape[1]
    n, top, rows = slot.shape
    weighted = cots is not None
    outs = [jax.ShapeDtypeStruct((rows + (16 if weighted else 0), half // cuts), BF)] * (n * cuts)
    ins = [slot, weight] + list(pieces) + (list(cots) if weighted else [])
    out = pl.pallas_call(
        functools.partial(join_kernel, n, cap, columns, weighted, cuts),
        out_shape=outs,
        in_specs=[VMEM] * len(ins),
        out_specs=[VMEM] * len(outs),
        scratch_shapes=[pltpu.VMEM((columns * cap, half), BF)],
        compiler_params=PARAMS,
        cost_estimate=LARGE,
        name="join_weighted" if weighted else "join",
    )(*ins)
    return list(out)


def halves(head_ref, half):
    head = head_ref[0]
    return (
        pl.ds(pl.multiple_of(head * half, half), half),
        pl.ds(pl.multiple_of((1 - head) * half, half), half),
    )


def ahead_kernel(
    half, head_ref, mine_ref, other_ref, gate_ref, up_ref, down_ref,
    pre_gate_ref, pre_up_ref, act_ref, kept_ref, sent_ref,
):
    own, away = halves(head_ref, half)
    mine, other = mine_ref[...], other_ref[...]
    pre_gate = dot(mine, gate_ref[own, :], 1, 0) + dot(other, gate_ref[away, :], 1, 0)
    pre_up = dot(mine, up_ref[own, :], 1, 0) + dot(other, up_ref[away, :], 1, 0)
    pre_gate_ref[...] = pre_gate
    pre_up_ref[...] = pre_up
    act = (pre_gate * (1.0 / (1.0 + jnp.exp(-pre_gate))) * pre_up).astype(BF)
    act_ref[...] = act
    sent_ref[...] = dot(act, down_ref[:, away], 1, 0).astype(BF)
    kept_ref[...] = dot(act, down_ref[:, own], 1, 0).astype(BF)


def back_kernel(
    half, head_ref, mine_ref, other_ref, pre_gate_ref, pre_up_ref, gate_ref, up_ref, down_ref,
    d_gate_ref, d_up_ref, kept_ref, sent_ref,
):
    own, away = halves(head_ref, half)
    d_act = dot(mine_ref[...], down_ref[:, own], 1, 1) + dot(other_ref[...], down_ref[:, away], 1, 1)
    pre_gate, pre_up = pre_gate_ref[...], pre_up_ref[...]
    sig = 1.0 / (1.0 + jnp.exp(-pre_gate))
    d_gate = (d_act * pre_up * sig * (1.0 + pre_gate * (1.0 - sig))).astype(BF)
    d_up = (d_act * (pre_gate * sig)).astype(BF)
    d_gate_ref[...] = d_gate
    d_up_ref[...] = d_up
    for span, ref in ((away, sent_ref), (own, kept_ref)):
        ref[...] = (dot(d_gate, gate_ref[span, :], 1, 1) + dot(d_up, up_ref[span, :], 1, 1)).astype(BF)


def by_rows(kernel, head, rows_in, whole_in, outs, name):
    total, half = rows_in[0].shape
    block = min(256, total)

    def cut(width):
        return pl.BlockSpec((block, width), lambda i: (i, 0))

    return pl.pallas_call(
        functools.partial(kernel, half),
        grid=(total // block,),
        out_shape=[jax.ShapeDtypeStruct((total, width), dtype) for width, dtype in outs],
        in_specs=[SMEM]
        + [cut(v.shape[1]) for v in rows_in]
        + [pl.BlockSpec(v.shape, lambda i: (0, 0)) for v in whole_in],
        out_specs=[cut(width) for width, _ in outs],
        compiler_params=PARAMS,
        cost_estimate=LARGE,
        name=name,
    )(head, *rows_in, *whole_in)


def deal_kernel(sizes, kept_ref, came_ref, *pieces):
    at = 0
    for piece, size in zip(pieces, sizes):
        total = kept_ref[at : at + size, :].astype(F32) + came_ref[at : at + size, :].astype(F32)
        piece[...] = total.astype(BF)
        at += size


def deal_rows(kept, came, sizes):
    return pl.pallas_call(
        functools.partial(deal_kernel, sizes),
        out_shape=[jax.ShapeDtypeStruct((size, kept.shape[1]), BF) for size in sizes],
        in_specs=[VMEM, VMEM],
        out_specs=[VMEM] * len(sizes),
        compiler_params=PARAMS,
        cost_estimate=SMALL,
        name="deal",
    )(kept, came)


def together(*values):
    return lax.optimization_barrier(values)


def shards(tokens, routes, combine_weights, w_gate, w_up, w_down, cotangent):
    columns, line = lax.axis_size("path"), lax.axis_size("expert")
    column, place, head = lax.axis_index("path"), lax.axis_index("expert"), lax.axis_index("head")
    tok_rows, half = tokens.shape
    top = routes.shape[1]
    groups = columns * line
    cap = max(2, 2 * tok_rows * top // groups)
    def after(value, *others):
        return together(value, *others)[0]

    flat = routes.reshape(-1)
    order = jnp.arange(flat.shape[0], dtype=jnp.int32)
    earlier = (flat[:, None] == flat[None, :]) & (order[:, None] < order[None, :])
    rank = jnp.sum(earlier.astype(jnp.int32), axis=0)
    position = (flat * cap + rank).astype(F32).reshape(tok_rows, top)
    about = jnp.concatenate([position.T, combine_weights.T], axis=0)

    def exchange(pieces):
        return [pieces[0]] + [
            lax.ppermute(pieces[d], "path", [(i, i ^ d) for i in range(columns)])
            for d in range(columns - 1, 0, -1)
        ][::-1]

    near, far = slice(0, line - 1), slice(line - 1, line)

    every = slice(0, line)

    def pick_group(got, part, scaled, cost=SMALL):
        blocks = [got[d] for d in range(line)[part]]
        return pick_rows(slot[part], weight[part], blocks, cap, columns, scaled, cost)

    first_bit = powers(line)[-1]
    info = jnp.stack([about] + [to_place(about, d, line) for d in range(1, line)], axis=0)
    where_to = info[:, :top].astype(jnp.int32)
    expert = where_to // cap
    slot = ((expert // line) ^ column) * cap + where_to % cap
    slot = jnp.where(expert % line == place, slot, -1)
    weight = info[:, top:]
    tok_in = line_gather(tokens, line, first=info)

    cot_far = after(cotangent, tok_in[first_bit])
    cot_near = after(cotangent, tok_in[line - 1])
    cot_in = line_gather(cot_near, line, cot_far)

    gate_cols, up_cols, down_rows = w_gate[0], w_up[0], w_down[0]
    head_arg = head.reshape(1).astype(jnp.int32)
    hidden = gate_cols.shape[1]

    def swap(value):
        return lax.ppermute(value, "head", SWAP)

    def full(mine, other):
        first = head == 0
        return jnp.concatenate(
            [jnp.where(first, mine, other), jnp.where(first, other, mine)], axis=1
        )

    tok_near = exchange(pick_group(tok_in, near, False))
    tok_in[line - 1] = after(tok_in[line - 1], *tok_near[1:])
    tok_far = exchange(pick_group(tok_in, far, False))
    tok_far[-1] = after(tok_far[-1], cot_in[first_bit], cot_in[1])
    tok_mine = stack_rows([p for pair in zip(tok_near, tok_far) for p in pair])
    cot_in[0] = after(cot_in[0], tok_mine)
    cot_near_rows = pick_group(cot_in, near, True)
    tok_other = after(swap(tok_mine), cot_near_rows[0])
    pre_gate, pre_up, activation, out_kept, out_sent = by_rows(
        ahead_kernel,
        head_arg,
        [tok_mine, tok_other],
        [gate_cols, up_cols, down_rows],
        [(hidden, F32), (hidden, F32), (hidden, BF), (half, BF), (half, BF)],
        "ahead",
    )
    cot_near_in = exchange(cot_near_rows)
    cot_in[line - 1] = after(cot_in[line - 1], out_sent)
    cot_far_rows = pick_group(cot_in, far, True, LARGE)
    out_came = after(swap(out_sent), cot_far_rows[0])
    out_pieces = deal_rows(out_kept, out_came, [cap * (line - 1), cap] * columns)
    cot_far_in = exchange(cot_far_rows)
    out_far = exchange(out_pieces[1::2])
    cot_mine = stack_rows([p for pair in zip(cot_near_in, cot_far_in) for p in pair])
    cots = [cot_in[d] for d in range(line)]
    out_far[-1] = after(out_far[-1], cot_mine)
    out_parts_far = join_rows(slot[far], weight[far], out_far, cap, cots[far])
    out_near = exchange(list(together(*out_pieces[::2], cot_mine)[:-1]))
    cot_other = after(swap(cot_mine), out_parts_far[0])
    d_pre_gate, d_pre_up, back_kept, back_sent = by_rows(
        back_kernel,
        head_arg,
        [cot_mine, cot_other, pre_gate, pre_up],
        [gate_cols, up_cols, down_rows],
        [(hidden, BF), (hidden, BF), (half, BF), (half, BF)],
        "back",
    )
    out_near[-1] = after(out_near[-1], back_sent)
    out_parts = join_rows(slot[near], weight[near], out_near, cap, cots[near]) + out_parts_far
    back_came = after(swap(back_sent), out_parts[0])
    first, last = slice(0, line - 2), slice(line - 2, line)
    back_pieces = deal_rows(back_kept, back_came, [cap * (line - 2), cap * 2] * columns)
    back_last = exchange(back_pieces[1::2])
    out_parts[0] = after(out_parts[0], *back_pieces)
    out_parts[line - 2] = after(out_parts[line - 2], *back_pieces)
    out_sums = dict(enumerate(out_parts))
    reduce_bit(out_sums, 1, line)
    back_last[-1] = after(back_last[-1], *out_sums.values())
    back_parts_last = join_rows(slot[last], weight[last], back_last, cap, cuts=2)
    back_first = exchange(
        [back_pieces[0]] + list(together(*back_pieces[2::2], *back_last[1:])[: columns - 1])
    )
    moved = [to_place(part, 1, line) for part in back_parts_last[2:]]

    d_pre_gate, d_pre_up, tok_mine, tok_other, _ = together(
        d_pre_gate, d_pre_up, tok_mine, tok_other, back_parts_last[0]
    )
    inbound = full(tok_mine, tok_other)
    grad_gate = dot(inbound, d_pre_gate, 0, 0).astype(BF)
    grad_up = dot(inbound, d_pre_up, 0, 0).astype(BF)

    back_first[-1] = after(back_first[-1], grad_gate)
    back_parts = join_rows(slot[first], weight[first], back_first, cap)
    moved[0] = after(moved[0], grad_gate, grad_up)
    back_cut = [(k.astype(F32) + m.astype(F32)).astype(BF) for k, m in zip(back_parts_last, moved)]
    back_pair = back_cut[1]
    activation, cot_mine, cot_other, _ = together(activation, cot_mine, cot_other, back_pair)
    grad_down = dot(activation, full(cot_mine, cot_other), 0, 0).astype(BF)

    out_sums[0] = after(out_sums[0], back_pair)
    for bit in powers(line)[1:]:
        reduce_bit(out_sums, bit, line)
    out_total = out_sums[0]
    back_parts[0] = after(back_parts[0], out_total)
    if line == 4:
        beside = to_place(back_parts[1], 1, line).astype(F32)
        across = jnp.concatenate([to_place(part, 2, line) for part in back_cut], axis=1)
        d_tokens = (back_parts[0].astype(F32) + beside + across.astype(F32)).astype(BF)
    else:
        back_sums = dict(enumerate(back_parts + [jnp.concatenate(back_cut, axis=1)]))
        for bit in powers(line):
            reduce_bit(back_sums, bit, line)
        d_tokens = back_sums[0]
    layer_out = out_total[:tok_rows]
    gate_terms = out_total[tok_rows, : 2 * top * tok_rows].astype(F32).reshape(2, top, tok_rows)
    local_gates = gate_terms[0] + gate_terms[1]
    d_gates = (local_gates + swap(local_gates)).T
    return (layer_out, d_tokens, d_gates, grad_gate[None], grad_up[None], grad_down[None])


def solution(mesh):
    rows = P(("path", "expert"), "head")
    whole = P(("path", "expert"), None)
    cols = P(("path", "expert"), None, "head")
    downs = P(("path", "expert"), "head", None)
    return jax.shard_map(
        shards,
        mesh=mesh,
        in_specs=(rows, whole, whole, cols, cols, downs, rows),
        out_specs=(rows, rows, whole, cols, cols, downs),
        check_vma=False,
    )
```

```python
import functools

import jax
import jax.numpy as jnp
from jax import lax
from jax.experimental import pallas as pl
from jax.experimental.pallas import tpu as pltpu
from jax.sharding import PartitionSpec as P

BF = jnp.bfloat16
F32 = jnp.float32
VMEM = pl.BlockSpec(memory_space=pltpu.VMEM)
SMEM = pl.BlockSpec(memory_space=pltpu.SMEM)
ANY = pl.BlockSpec(memory_space=pl.ANY)
PARAMS = pltpu.CompilerParams(vmem_limit_bytes=48 << 20)
SWAP = [(0, 1), (1, 0)]
LARGE = pl.CostEstimate(flops=400_000_000_000, bytes_accessed=40 << 20, transcendentals=0)
SMALL = pl.CostEstimate(flops=0, bytes_accessed=0, transcendentals=0)


def dot(a, b, ca, cb):
    return lax.dot_general(a, b, (((ca,), (cb,)), ((), ())), preferred_element_type=F32)


def powers(line):
    bits = [1]
    while bits[-1] * 2 < line:
        bits.append(bits[-1] * 2)
    return bits


def to_place(value, d, line):
    return lax.ppermute(value, "expert", [(i, i ^ d) for i in range(line)])


def line_gather(block, line, early=None, first=None):
    got = {0: block}
    for bit in reversed(powers(line)):
        for d in list(got):
            if d | bit in got:
                continue
            sent = early if early is not None and len(got) == 1 else got[d]
            got[d | bit] = to_place(sent, bit, line)
            if first is not None and d == 0 and bit == powers(line)[-1]:
                got[bit], _, got[1] = together(got[bit], first, to_place(block, 1, line))
    return got


def reduce_bit(parts, bit, line):
    for d in sorted((d for d in parts if d & bit), reverse=True):
        moved = to_place(parts.pop(d), bit, line)
        kept = parts[d ^ bit].astype(F32) + moved.astype(F32)
        parts[d ^ bit] = kept.astype(moved.dtype)


def pick_kernel(n, cap, columns, scaled, *refs):
    slot_ref, weight_ref = refs[:2]
    blocks, pieces = refs[2 : 2 + n], refs[2 + n :]
    slots = columns * cap
    for j in range(n):
        block = blocks[j][...]
        ids = lax.broadcasted_iota(jnp.int32, (slots, block.shape[0]), 0)
        hits = [ids == slot_ref[j, k : k + 1, :] for k in range(slot_ref.shape[1])]
        pick = functools.reduce(jnp.add, [h.astype(F32) for h in hits]).astype(BF)
        rows = dot(pick, block, 1, 0)
        if scaled:
            given = functools.reduce(
                jnp.add,
                [jnp.where(h, weight_ref[j, k : k + 1, :], 0.0) for k, h in enumerate(hits)],
            )
            rows = rows * jnp.sum(given, axis=1, keepdims=True)
        rows = rows.astype(BF)
        for d in range(columns):
            pieces[d][j * cap : (j + 1) * cap, :] = rows[d * cap : (d + 1) * cap, :]


def pick_rows(slot, weight, blocks, cap, columns, scaled, cost):
    rows, half = blocks[0].shape
    n = len(blocks)
    return list(pl.pallas_call(
        functools.partial(pick_kernel, n, cap, columns, scaled),
        out_shape=[jax.ShapeDtypeStruct((n * cap, half), BF)] * columns,
        in_specs=[VMEM] * (2 + n),
        out_specs=[VMEM] * columns,
        compiler_params=PARAMS,
        cost_estimate=cost,
        name="pick_scaled" if scaled else "pick",
    )(slot, weight, *blocks))


def stack_kernel(count, *refs):
    pieces, out = refs[:count], refs[count]
    at = 0
    for piece in pieces:
        size = piece.shape[0]
        out[at : at + size, :] = piece[...]
        at += size


def stack_rows(pieces):
    total = sum(p.shape[0] for p in pieces)
    half = pieces[0].shape[1]
    return pl.pallas_call(
        functools.partial(stack_kernel, len(pieces)),
        out_shape=jax.ShapeDtypeStruct((total, half), BF),
        in_specs=[VMEM] * len(pieces),
        out_specs=VMEM,
        compiler_params=PARAMS,
        cost_estimate=SMALL,
        name="stack",
    )(*pieces)


def join_kernel(n, cap, columns, weighted, cuts, *refs):
    slot_ref, weight_ref = refs[:2]
    pieces, rest = refs[2 : 2 + columns], refs[2 + columns :]
    held = rest[-1]
    if weighted:
        cots, parts = rest[:n], rest[n : 2 * n]
    else:
        parts = rest[: n * cuts]
    slots = columns * cap
    top = slot_ref.shape[1]
    for j in range(n):
        for d in range(columns):
            held[d * cap : (d + 1) * cap, :] = pieces[d][j * cap : (j + 1) * cap, :]
        rows = held[...]
        ids = lax.broadcasted_iota(jnp.int32, (slots, slot_ref.shape[2]), 0)
        hits = [ids == slot_ref[j, k : k + 1, :] for k in range(top)]
        if weighted:
            given = functools.reduce(
                jnp.add,
                [jnp.where(h, weight_ref[j, k : k + 1, :], 0.0) for k, h in enumerate(hits)],
            )
            high = given.astype(BF)
            low = (given - high.astype(F32)).astype(BF)
            parts[j][: high.shape[1], :] = (dot(high, rows, 0, 0) + dot(low, rows, 0, 0)).astype(BF)
            meet = dot(rows, cots[j][...], 1, 1)
            width = meet.shape[1]
            for k, h in enumerate(hits):
                gate = jnp.sum(jnp.where(h, meet, 0.0), axis=0, keepdims=True)
                gate_high = gate.astype(BF)
                gate_low = (gate - gate_high.astype(F32)).astype(BF)
                for half_at, value in ((0, gate_high), (top, gate_low)):
                    at = (half_at + k) * width
                    parts[j][width : width + 16, at : at + width] = jnp.broadcast_to(value, (16, width))
        else:
            pick = functools.reduce(jnp.add, [h.astype(F32) for h in hits]).astype(BF)
            total = dot(pick, rows, 0, 0).astype(BF)
            width = total.shape[1] // cuts
            for s in range(cuts):
                parts[j * cuts + s][...] = total[:, s * width : (s + 1) * width]


def join_rows(slot, weight, pieces, cap, cots=None, cuts=1):
    columns, half = len(pieces), pieces[0].shape[1]
    n, top, rows = slot.shape
    weighted = cots is not None
    outs = [jax.ShapeDtypeStruct((rows + (16 if weighted else 0), half // cuts), BF)] * (n * cuts)
    ins = [slot, weight] + list(pieces) + (list(cots) if weighted else [])
    out = pl.pallas_call(
        functools.partial(join_kernel, n, cap, columns, weighted, cuts),
        out_shape=outs,
        in_specs=[VMEM] * len(ins),
        out_specs=[VMEM] * len(outs),
        scratch_shapes=[pltpu.VMEM((columns * cap, half), BF)],
        compiler_params=PARAMS,
        cost_estimate=LARGE,
        name="join_weighted" if weighted else "join",
    )(*ins)
    return list(out)


def halves(head_ref, half):
    head = head_ref[0]
    return (
        pl.ds(pl.multiple_of(head * half, half), half),
        pl.ds(pl.multiple_of((1 - head) * half, half), half),
    )


def ahead_kernel(
    half, head_ref, mine_ref, other_ref, gate_ref, up_ref, down_ref,
    pre_gate_ref, pre_up_ref, act_ref, kept_ref, sent_ref,
):
    own, away = halves(head_ref, half)
    mine, other = mine_ref[...], other_ref[...]
    pre_gate = dot(mine, gate_ref[own, :], 1, 0) + dot(other, gate_ref[away, :], 1, 0)
    pre_up = dot(mine, up_ref[own, :], 1, 0) + dot(other, up_ref[away, :], 1, 0)
    pre_gate_ref[...] = pre_gate
    pre_up_ref[...] = pre_up
    act = (pre_gate * (1.0 / (1.0 + jnp.exp(-pre_gate))) * pre_up).astype(BF)
    act_ref[...] = act
    sent_ref[...] = dot(act, down_ref[:, away], 1, 0).astype(BF)
    kept_ref[...] = dot(act, down_ref[:, own], 1, 0).astype(BF)


def back_kernel(
    half, head_ref, mine_ref, other_ref, pre_gate_ref, pre_up_ref, gate_ref, up_ref, down_ref,
    d_gate_ref, d_up_ref, kept_ref, sent_ref,
):
    own, away = halves(head_ref, half)
    d_act = dot(mine_ref[...], down_ref[:, own], 1, 1) + dot(other_ref[...], down_ref[:, away], 1, 1)
    pre_gate, pre_up = pre_gate_ref[...], pre_up_ref[...]
    sig = 1.0 / (1.0 + jnp.exp(-pre_gate))
    d_gate = (d_act * pre_up * sig * (1.0 + pre_gate * (1.0 - sig))).astype(BF)
    d_up = (d_act * (pre_gate * sig)).astype(BF)
    d_gate_ref[...] = d_gate
    d_up_ref[...] = d_up
    for span, ref in ((away, sent_ref), (own, kept_ref)):
        ref[...] = (dot(d_gate, gate_ref[span, :], 1, 1) + dot(d_up, up_ref[span, :], 1, 1)).astype(BF)


def by_rows(kernel, head, rows_in, whole_in, outs, name):
    total, half = rows_in[0].shape
    block = min(512, total)

    def cut(width):
        return pl.BlockSpec((block, width), lambda i: (i, 0))

    return pl.pallas_call(
        functools.partial(kernel, half),
        grid=(total // block,),
        out_shape=[jax.ShapeDtypeStruct((total, width), dtype) for width, dtype in outs],
        in_specs=[SMEM]
        + [cut(v.shape[1]) for v in rows_in]
        + [pl.BlockSpec(v.shape, lambda i: (0, 0)) for v in whole_in],
        out_specs=[cut(width) for width, _ in outs],
        compiler_params=PARAMS,
        cost_estimate=LARGE,
        name=name,
    )(head, *rows_in, *whole_in)


def deal_kernel(sizes, kept_ref, came_ref, *pieces):
    at = 0
    for piece, size in zip(pieces, sizes):
        total = kept_ref[at : at + size, :].astype(F32) + came_ref[at : at + size, :].astype(F32)
        piece[...] = total.astype(BF)
        at += size


def deal_rows(kept, came, sizes):
    return pl.pallas_call(
        functools.partial(deal_kernel, sizes),
        out_shape=[jax.ShapeDtypeStruct((size, kept.shape[1]), BF) for size in sizes],
        in_specs=[VMEM, VMEM],
        out_specs=[VMEM] * len(sizes),
        compiler_params=PARAMS,
        cost_estimate=SMALL,
        name="deal",
    )(kept, came)


def together(*values):
    return lax.optimization_barrier(values)


def shards(tokens, routes, combine_weights, w_gate, w_up, w_down, cotangent):
    columns, line = lax.axis_size("path"), lax.axis_size("expert")
    column, place, head = lax.axis_index("path"), lax.axis_index("expert"), lax.axis_index("head")
    tok_rows, half = tokens.shape
    top = routes.shape[1]
    groups = columns * line
    cap = max(2, 2 * tok_rows * top // groups)
    def after(value, *others):
        return together(value, *others)[0]

    flat = routes.reshape(-1)
    order = jnp.arange(flat.shape[0], dtype=jnp.int32)
    earlier = (flat[:, None] == flat[None, :]) & (order[:, None] < order[None, :])
    rank = jnp.sum(earlier.astype(jnp.int32), axis=0)
    position = (flat * cap + rank).astype(F32).reshape(tok_rows, top)
    about = jnp.concatenate([position.T, combine_weights.T], axis=0)

    def exchange(pieces):
        return [pieces[0]] + [
            lax.ppermute(pieces[d], "path", [(i, i ^ d) for i in range(columns)])
            for d in range(columns - 1, 0, -1)
        ][::-1]

    near, far = slice(0, line - 1), slice(line - 1, line)

    every = slice(0, line)

    def pick_group(got, part, scaled, cost=SMALL):
        blocks = [got[d] for d in range(line)[part]]
        return pick_rows(slot[part], weight[part], blocks, cap, columns, scaled, cost)

    first_bit = powers(line)[-1]
    info = jnp.stack([about] + [to_place(about, d, line) for d in range(1, line)], axis=0)
    where_to = info[:, :top].astype(jnp.int32)
    expert = where_to // cap
    slot = ((expert // line) ^ column) * cap + where_to % cap
    slot = jnp.where(expert % line == place, slot, -1)
    weight = info[:, top:]
    tok_in = line_gather(tokens, line, first=info)

    cot_far = after(cotangent, tok_in[first_bit])
    cot_near = after(cotangent, tok_in[line - 1])
    cot_in = line_gather(cot_near, line, cot_far)

    gate_cols, up_cols, down_rows = w_gate[0], w_up[0], w_down[0]
    head_arg = head.reshape(1).astype(jnp.int32)
    hidden = gate_cols.shape[1]

    def swap(value):
        return lax.ppermute(value, "head", SWAP)

    def full(mine, other):
        first = head == 0
        return jnp.concatenate(
            [jnp.where(first, mine, other), jnp.where(first, other, mine)], axis=1
        )

    tok_near = exchange(pick_group(tok_in, near, False))
    tok_in[line - 1] = after(tok_in[line - 1], *tok_near[1:])
    tok_far = exchange(pick_group(tok_in, far, False))
    tok_far[-1] = after(tok_far[-1], cot_in[first_bit], cot_in[1])
    tok_mine = stack_rows([p for pair in zip(tok_near, tok_far) for p in pair])
    cot_in[0] = after(cot_in[0], tok_mine)
    cot_near_rows = pick_group(cot_in, near, True)
    tok_other = after(swap(tok_mine), cot_near_rows[0])
    pre_gate, pre_up, activation, out_kept, out_sent = by_rows(
        ahead_kernel,
        head_arg,
        [tok_mine, tok_other],
        [gate_cols, up_cols, down_rows],
        [(hidden, F32), (hidden, F32), (hidden, BF), (half, BF), (half, BF)],
        "ahead",
    )
    cot_near_in = exchange(cot_near_rows)
    cot_in[line - 1] = after(cot_in[line - 1], out_sent)
    cot_far_rows = pick_group(cot_in, far, True, LARGE)
    out_came = after(swap(out_sent), cot_far_rows[0])
    out_pieces = deal_rows(out_kept, out_came, [cap * (line - 1), cap] * columns)
    cot_far_in = exchange(cot_far_rows)
    out_far = exchange(out_pieces[1::2])
    cot_mine = stack_rows([p for pair in zip(cot_near_in, cot_far_in) for p in pair])
    cots = [cot_in[d] for d in range(line)]
    out_far[-1] = after(out_far[-1], cot_mine)
    out_parts_far = join_rows(slot[far], weight[far], out_far, cap, cots[far])
    out_near = exchange(list(together(*out_pieces[::2], cot_mine)[:-1]))
    cot_other = after(swap(cot_mine), out_parts_far[0])
    d_pre_gate, d_pre_up, back_kept, back_sent = by_rows(
        back_kernel,
        head_arg,
        [cot_mine, cot_other, pre_gate, pre_up],
        [gate_cols, up_cols, down_rows],
        [(hidden, BF), (hidden, BF), (half, BF), (half, BF)],
        "back",
    )
    out_near[-1] = after(out_near[-1], back_sent)
    out_parts = join_rows(slot[near], weight[near], out_near, cap, cots[near]) + out_parts_far
    back_came = after(swap(back_sent), out_parts[0])
    first, last = slice(0, line - 2), slice(line - 2, line)
    back_pieces = deal_rows(back_kept, back_came, [cap * (line - 2), cap * 2] * columns)
    back_last = exchange(back_pieces[1::2])
    out_parts[0] = after(out_parts[0], *back_pieces)
    out_parts[line - 2] = after(out_parts[line - 2], *back_pieces)
    out_sums = dict(enumerate(out_parts))
    reduce_bit(out_sums, 1, line)
    back_last[-1] = after(back_last[-1], *out_sums.values())
    back_parts_last = join_rows(slot[last], weight[last], back_last, cap, cuts=2)
    back_first = exchange(
        [back_pieces[0]] + list(together(*back_pieces[2::2], *back_last[1:])[: columns - 1])
    )
    moved = [to_place(part, 1, line) for part in back_parts_last[2:]]

    d_pre_gate, d_pre_up, tok_mine, tok_other, _ = together(
        d_pre_gate, d_pre_up, tok_mine, tok_other, back_parts_last[0]
    )
    inbound = full(tok_mine, tok_other)
    grad_gate = dot(inbound, d_pre_gate, 0, 0).astype(BF)
    grad_up = dot(inbound, d_pre_up, 0, 0).astype(BF)

    back_first[-1] = after(back_first[-1], grad_gate)
    back_parts = join_rows(slot[first], weight[first], back_first, cap)
    moved[0] = after(moved[0], grad_gate)
    back_cut = [(k.astype(F32) + m.astype(F32)).astype(BF) for k, m in zip(back_parts_last, moved)]
    back_pair = back_cut[1]
    activation, cot_mine, cot_other, _ = together(activation, cot_mine, cot_other, back_pair)
    grad_down = dot(activation, full(cot_mine, cot_other), 0, 0).astype(BF)

    out_sums[0] = after(out_sums[0], back_pair)
    for bit in powers(line)[1:]:
        reduce_bit(out_sums, bit, line)
    out_total = out_sums[0]
    back_parts[0] = after(back_parts[0], out_total)
    if line == 4:
        beside = to_place(back_parts[1], 1, line).astype(F32)
        across = jnp.concatenate([to_place(part, 2, line) for part in back_cut], axis=1)
        d_tokens = (back_parts[0].astype(F32) + beside + across.astype(F32)).astype(BF)
    else:
        back_sums = dict(enumerate(back_parts + [jnp.concatenate(back_cut, axis=1)]))
        for bit in powers(line):
            reduce_bit(back_sums, bit, line)
        d_tokens = back_sums[0]
    layer_out = out_total[:tok_rows]
    gate_terms = out_total[tok_rows, : 2 * top * tok_rows].astype(F32).reshape(2, top, tok_rows)
    local_gates = gate_terms[0] + gate_terms[1]
    d_gates = (local_gates + swap(local_gates)).T
    return (layer_out, d_tokens, d_gates, grad_gate[None], grad_up[None], grad_down[None])


def solution(mesh):
    rows = P(("path", "expert"), "head")
    whole = P(("path", "expert"), None)
    cols = P(("path", "expert"), None, "head")
    downs = P(("path", "expert"), "head", None)
    return jax.shard_map(
        shards,
        mesh=mesh,
        in_specs=(rows, whole, whole, cols, cols, downs, rows),
        out_specs=(rows, rows, whole, cols, cols, downs),
        check_vma=False,
    )
```
